256 devices in a mesh: cell: 16 (over x, z_lo, core), gene: 16 (over y, z_hi).
Axes of the slice: x: 4, y: 4, z: 8 (z_hi: 4, z_lo: 2; z = z_hi * 2 + z_lo), core: 2. Of those that a mesh axis runs over, the one named last changes fastest.
Arguments:
- query_rows: bfloat16 [16, 2048, 1536], P('cell', 'gene'), may hold values from -1.5 to 1.5
- key_rows: bfloat16 [16, 2048, 1536], P('cell', 'gene'), may hold values from -1.5 to 1.5
- value_rows: bfloat16 [16, 2048, 1536], P('cell', 'gene'), may hold values from -6 to 6
- output_rows: bfloat16 [16, 2048, 1536], P('cell', 'gene'), may hold values from -6 to 6
- output_grad: bfloat16 [16, 2048, 1536], P('cell', 'gene'), may hold values from -6 to 6
- row_lse: float32 [16, 2048, 12], P('cell', 'gene'), may hold values from 3 to 6
- block_bias: float32 [16, 12, 16], replicated, may hold values from -1.5 to 1.5
- block_index: int32 [16, 16], replicated, may hold values from 0 to 15, each once within a row
- block_count: int32 [16], replicated, may hold values from 1 to 16, 128 in all
Outputs:
- query_grad: bfloat16 [16, 2048, 1536], P('cell', 'gene')
- key_grad: bfloat16 [16, 2048, 1536], P('cell', 'gene')
- value_grad: bfloat16 [16, 2048, 1536], P('cell', 'gene')
- bias_grad: float32 [16, 12, 16], P('gene', None, 'cell')
The draws below stay inside these ranges and needn't reach their ends.
Inputs may be any that keep to these rules, and one draw needn't show every extreme that they name: Each row of block_index lists every key block once; its first block_count entries are the listed ones, and one row block lists all 16. `block_count`: one row block has 16 listed key blocks.
All inputs are finite; a program needn't handle non-finite values.
Results may differ from the reference program's by a relative error of at most 0.0049.
Values may be sent and summed in bfloat16 or wider, within the bound.
A program may use at most 128 MiB of HBM per device.

```python
import math
import jax
import jax.numpy as jnp
import numpy as np
from jax import lax

BLOCK = 128
HEADS = 12
HEAD_DIM = 128
NB = 16
GENES = 2048
CELLS = 16


def block_levels(own_key, extent, pieces, least, largest):
    factor_of = 1.0
    for axis_at, parts in pieces:
        draws = jax.random.uniform(jax.random.fold_in(jax.random.fold_in(own_key, 6), axis_at), (parts,), jnp.float32, least / len(pieces), largest / len(pieces))
        factor_of = factor_of * jnp.repeat(jnp.exp(draws), extent[axis_at] // parts).reshape((-1,) + (1,) * (len(extent) - 1 - axis_at))
    return factor_of


def profile(count, total, bound, slope):
    portions = [(1 << 20) // math.isqrt(standing ** slope) + 1 for standing in range(2, count + 1)]
    spare, given = total - bound - (count - 1), [1] * (count - 1)
    while spare > 0:
        movable = [i for i in range(count - 1) if given[i] < bound]
        whole, budget = sum([portions[i] for i in movable]), spare
        for i in movable:
            extra = min(bound - given[i], max(1, budget * portions[i] // whole), spare)
            given[i] = given[i] + extra
            spare = spare - extra
    return np.array([bound] + given)


def uneven(rng, number_of, total, bound, lean):
    if number_of == 2:
        one = jax.random.randint(rng, (), max(1, total - bound), min(bound, total - 1) + 1)
        return jnp.stack([one, total - one])
    tallies = jnp.asarray(profile(number_of, total, bound, lean), jnp.int32)
    pairs = (number_of - 1) // 2
    source_of, receiver = tallies[1:1 + 2 * pairs:2], tallies[2:2 + 2 * pairs:2]
    slack = jnp.minimum(source_of - 1, bound - receiver)
    passed = jax.random.randint(jax.random.fold_in(rng, 1), (pairs,), 0, 1 << 20) % (slack + 1)
    tallies = tallies.at[1:1 + 2 * pairs:2].set(source_of - passed).at[2:2 + 2 * pairs:2].set(receiver + passed)
    return tallies[jax.random.permutation(jax.random.fold_in(rng, 2), number_of)]


def centred(stream_key, shape, spread, bound, split=(), kind=jnp.bfloat16):
    loudness = block_levels(stream_key, shape, split, -0.22, 0.18) if split else 1.0
    entries = jax.random.normal(stream_key, shape, jnp.float32) * spread * loudness
    return jnp.minimum(jnp.maximum(entries, -bound), bound).astype(kind)


def setup_inputs(seed: int = 0) -> dict:
    key_of = jax.random.split(jax.random.key(seed), 10)
    query_rows = jnp.clip(jax.random.uniform(key_of[0], (CELLS, GENES, HEADS * HEAD_DIM), jnp.float32, -1.5, 1.5) * block_levels(key_of[0], (CELLS, GENES, HEADS * HEAD_DIM), ((0, 16), (1, 16)), -0.4, 0.0), -1.5, 1.5).astype(jnp.bfloat16)
    key_rows = jnp.clip(jax.random.uniform(key_of[1], (CELLS, GENES, HEADS * HEAD_DIM), jnp.float32, -1.5, 1.5) * block_levels(key_of[1], (CELLS, GENES, HEADS * HEAD_DIM), ((0, 16), (1, 16)), -0.4, 0.0), -1.5, 1.5).astype(jnp.bfloat16)
    value_rows = centred(key_of[2], (CELLS, GENES, HEADS * HEAD_DIM), 1.0, 6.0, ((0, 16), (1, 16)))
    output_rows = centred(key_of[3], (CELLS, GENES, HEADS * HEAD_DIM), 1.0, 6.0, ((0, 16), (1, 16)))
    output_grad = centred(key_of[4], (CELLS, GENES, HEADS * HEAD_DIM), 1.0, 6.0, ((0, 16), (1, 16)))
    row_lse = jnp.clip(3.0 + 3.0 * jax.random.uniform(key_of[5], (CELLS, GENES, HEADS), jnp.float32) ** block_levels(key_of[5], (CELLS, GENES, HEADS), ((0, 16), (1, 16)), -0.2, 0.2), 3.0, 6.0)
    block_bias = jnp.clip(jax.random.uniform(key_of[6], (NB, HEADS, NB), jnp.float32, -1.5, 1.5), -1.5, 1.5)
    block_index = jax.vmap(lambda own: jax.random.permutation(own, NB))(jax.random.split(key_of[7], NB)).reshape((NB, NB)).astype(jnp.int32)
    block_count = uneven(key_of[8], NB, NB * NB // 2, NB, 2).astype(jnp.int32)
    return dict(query_rows=query_rows, key_rows=key_rows, value_rows=value_rows, output_rows=output_rows, output_grad=output_grad, row_lse=row_lse, block_bias=block_bias, block_index=block_index, block_count=block_count)


def pair_tables(block_bias, block_index, block_count):
    block_total = block_bias.shape[0]
    columns = jnp.arange(block_total, dtype=jnp.int32)
    slot_live = jnp.arange(block_index.shape[1], dtype=jnp.int32)[None, :] < block_count[:, None]
    listed = ((block_index[:, :, None] == columns[None, None, :]) & slot_live[:, :, None]).astype(jnp.float32)
    pair_bias = jnp.einsum('ihs,isj->hij', block_bias, listed, precision=lax.Precision.HIGHEST)
    pair_mask = lax.optimization_barrier(jnp.sum(listed, axis=1))
    return (listed, pair_bias, pair_mask)

def reference(query_rows, key_rows, value_rows, output_rows, output_grad, row_lse, block_bias, block_index, block_count):
    score_scale = 1.0 / math.sqrt(HEAD_DIM)
    listed, pair_bias, pair_mask = pair_tables(block_bias, block_index, block_count)
    full_bias = jnp.repeat(jnp.repeat(pair_bias, BLOCK, axis=1), BLOCK, axis=2)
    full_mask = jnp.repeat(jnp.repeat(pair_mask, BLOCK, axis=0), BLOCK, axis=1) > 0.5

    def one_cell(inputs):
        query, keyset, valueset, output, grad, lse = inputs
        shape = (GENES, HEADS, HEAD_DIM)
        query = query.astype(jnp.float32).reshape(shape)
        keyset = keyset.astype(jnp.float32).reshape(shape)
        valueset = valueset.astype(jnp.float32).reshape(shape)
        output = output.astype(jnp.float32).reshape(shape)
        grad = grad.astype(jnp.float32).reshape(shape)
        scores = jnp.einsum('rhd,khd->hrk', query, keyset) * score_scale + full_bias
        weights = jnp.where(full_mask[None], jnp.exp(scores - jnp.transpose(lse)[:, :, None]), 0.0)
        row_delta = jnp.transpose(lax.optimization_barrier(jnp.sum(grad * output, axis=-1)))
        weight_grads = jnp.einsum('rhd,khd->hrk', grad, valueset)
        score_grads = weights * (weight_grads - row_delta[:, :, None])
        weights_low = lax.optimization_barrier(weights.astype(jnp.bfloat16)).astype(jnp.float32)
        grads_low = lax.optimization_barrier(score_grads.astype(jnp.bfloat16)).astype(jnp.float32)
        value_grad = jnp.einsum('hrk,rhd->khd', weights_low, grad)
        query_grad = jnp.einsum('hrk,khd->rhd', grads_low, keyset) * score_scale
        key_grad = jnp.einsum('hrk,rhd->khd', grads_low, query) * score_scale
        block_sums = score_grads.reshape(HEADS, NB, BLOCK, NB, BLOCK).sum(axis=(2, 4))
        flat = (GENES, HEADS * HEAD_DIM)
        return (query_grad.reshape(flat).astype(jnp.bfloat16), key_grad.reshape(flat).astype(jnp.bfloat16), value_grad.reshape(flat).astype(jnp.bfloat16), block_sums)
    query_grad, key_grad, value_grad, block_sums = lax.map(one_cell, (query_rows, key_rows, value_rows, output_rows, output_grad, row_lse))
    bias_grad = jnp.einsum('hij,isj->ihs', lax.optimization_barrier(jnp.sum(block_sums, axis=0)), listed, precision=lax.Precision.HIGHEST)
    return (query_grad, key_grad, value_grad, bias_grad)
```

```python
import functools
import math

import jax
import jax.numpy as jnp
from jax import lax
from jax.experimental import pallas as pl
from jax.experimental.pallas import tpu as pltpu
from jax.sharding import PartitionSpec as P

MESH = pl.DeviceIdType.MESH
BLOCK = 128
SIDE = 4
CHUNK = 512
LOG2E = 1.4426950408889634
OFF = -1.0e30
BF16 = jnp.bfloat16
F32 = jnp.float32


def nt_dot(a, b):
    return lax.dot_general(a, b, (((1,), (1,)), ((), ())), preferred_element_type=F32)


def nn_dot(a, b):
    return jnp.dot(a, b, preferred_element_type=F32)


def kernel(
    heads,
    genes,
    cells,
    q_in,
    k_in,
    v_in,
    o_in,
    g_in,
    lse_in,
    bias_in,
    index_in,
    count_in,
    dq_out,
    dk_out,
    dv_out,
    bias_out,
    qf,
    kf,
    vf,
    gf,
    statf,
    o_own,
    g_own,
    stat,
    square,
    kt,
    addend,
    weights,
    grads,
    colsum,
    dq,
    dk,
    dv,
    terms,
    mine,
    packed,
    everyones,
    load_sem,
    in_send,
    in_recv,
    out_send,
    out_recv,
    term_send,
    term_recv,
    cell_send,
    cell_recv,
):
    gene = lax.axis_index("gene")
    cell = lax.axis_index("cell")
    row, col = gene // SIDE, gene % SIDE
    turn = 2 * (cell % 2) + (cell // 2) % 2
    live_heads = heads // SIDE
    scale = 1.0 / math.sqrt(BLOCK)

    def slot_of(r, c):
        return (r + c + turn) % SIDE

    place = slot_of(row, col)
    active = place < live_heads
    head = live_heads * col + place
    head_cols = pl.ds(pl.multiple_of(head * BLOCK, BLOCK), BLOCK)

    def peer(step):
        r, c = (row + step // SIDE) % SIDE, (col + step % SIDE) % SIDE
        return r, c, r * SIDE + c

    def block_of(i):
        return pl.ds(pl.multiple_of(i * BLOCK, BLOCK), BLOCK)

    barrier = pltpu.get_barrier_semaphore()
    for step in range(1, genes):
        pl.semaphore_signal(barrier, inc=1, device_id={"gene": peer(step)[2]}, device_id_type=MESH)
    for step in range(1, cells):
        pl.semaphore_signal(
            barrier, inc=1, device_id={"cell": (cell + step) % cells}, device_id_type=MESH
        )

    load_o = pltpu.make_async_copy(o_in.at[0], o_own, load_sem.at[0])
    load_g = pltpu.make_async_copy(g_in.at[0], g_own, load_sem.at[1])
    load_o.start()
    load_g.start()
    stat[...] = jnp.zeros_like(stat)
    square[...] = jnp.zeros_like(square)
    terms[...] = jnp.zeros_like(terms)
    packed[...] = jnp.zeros_like(packed)
    square[:, 0:heads] = lse_in[0]
    lanes = lax.broadcasted_iota(jnp.int32, (BLOCK, BLOCK), 1)
    turned = square[...].T
    for h in range(heads):
        stat[h, 0:1, :] = turned[h : h + 1, :]
    load_o.wait()
    load_g.wait()
    deltas = jnp.zeros((BLOCK, BLOCK), F32)
    for h in range(heads):
        cols = slice(h * BLOCK, (h + 1) * BLOCK)
        one = jnp.sum(
            g_own[:, cols].astype(F32) * o_own[:, cols].astype(F32), axis=1, keepdims=True
        )
        deltas = jnp.where(lanes == h, one, deltas)
    turned = deltas.T
    for h in range(heads):
        stat[h, 1:2, :] = turned[h : h + 1, :]

    pl.semaphore_wait(barrier, genes + cells - 2)

    moved = ((k_in, kf), (q_in, qf), (g_in, gf), (v_in, vf))

    def send_array(a, src, dst):
        for step in range(1, genes):
            r, c, to = peer(step)
            spot = slot_of(r, c)

            @pl.when(spot < live_heads)
            def _():
                cols = pl.ds(pl.multiple_of((live_heads * c + spot) * BLOCK, BLOCK), BLOCK)
                pltpu.make_async_remote_copy(
                    src_ref=src.at[0, :, cols],
                    dst_ref=dst.at[block_of(gene), :],
                    send_sem=in_send.at[a],
                    recv_sem=in_recv.at[a],
                    device_id={"gene": to},
                    device_id_type=MESH,
                ).start()

        @pl.when(active)
        def _():
            pltpu.make_async_copy(
                src.at[0, :, head_cols], dst.at[block_of(gene), :], in_recv.at[a]
            ).start()

    send_array(0, *moved[0])
    send_array(1, *moved[1])
    for step in range(1, genes):
        r, c, to = peer(step)
        spot = slot_of(r, c)

        @pl.when(spot < live_heads)
        def _():
            pltpu.make_async_remote_copy(
                src_ref=stat.at[live_heads * c + spot],
                dst_ref=statf.at[gene],
                send_sem=in_send.at[4],
                recv_sem=in_recv.at[4],
                device_id={"gene": to},
                device_id_type=MESH,
            ).start()

    @pl.when(active)
    def _():
        pltpu.make_async_copy(stat.at[head], statf.at[gene], in_recv.at[4]).start()

    send_array(2, *moved[2])
    send_array(3, *moved[3])

    def arrived(ref, sem):
        pltpu.make_async_copy(ref, ref, sem).wait()

    def give_back(a, src, dst, step):
        _, _, to = peer(step)

        @pl.when(to == gene)
        def _():
            pltpu.make_async_copy(
                src.at[block_of(to), :], dst.at[0, :, head_cols], out_recv.at[a]
            ).start()

        @pl.when(to != gene)
        def _():
            pltpu.make_async_remote_copy(
                src_ref=src.at[block_of(to), :],
                dst_ref=dst.at[0, :, head_cols],
                send_sem=out_send.at[a],
                recv_sem=out_recv.at[a],
                device_id={"gene": to},
                device_id_type=MESH,
            ).start()

    keys_iota = lax.broadcasted_iota(jnp.int32, (genes, genes), 0)
    slot_iota = lax.broadcasted_iota(jnp.int32, (genes, genes), 1)

    def listed(i):
        return (index_in[i : i + 1, :] == keys_iota) & (slot_iota < count_in[i])

    @pl.when(active)
    def _():
        arrived(statf, in_recv.at[4])
        for i in range(genes):
            hit = listed(i)
            bias_row = bias_in[i, pl.ds(head, 1), :]
            bias_col = jnp.sum(jnp.where(hit, bias_row, 0.0), axis=1, keepdims=True)
            hit_col = jnp.sum(jnp.where(hit, 1.0, 0.0), axis=1, keepdims=True)
            start = jnp.where(hit_col > 0.5, bias_col * LOG2E, OFF)
            addend[:, i * BLOCK : (i + 1) * BLOCK] = start - statf[i, 0:1, :] * LOG2E
        arrived(kf, in_recv.at[0])

        def turn_keys(i, carry):
            kt[:, block_of(i)] = kf[block_of(i), :].T
            return carry

        lax.fori_loop(0, genes, turn_keys, 0)
        arrived(qf, in_recv.at[1])
        arrived(gf, in_recv.at[2])

        def value_step(step, carry):
            _, _, j = peer(step)
            own = kf[block_of(j), :]
            total = jnp.zeros((BLOCK, BLOCK), F32)
            for n in range(genes * BLOCK // CHUNK):
                span = slice(n * CHUNK, (n + 1) * CHUNK)
                scores = nt_dot(own, qf[span, :])
                w = jnp.exp2(scores * (scale * LOG2E) + addend[pl.ds(j, 1), span])
                weights[block_of(j), span] = w
                total = total + nn_dot(w.astype(BF16), gf[span, :])
            dv[block_of(j), :] = total.astype(BF16)

            @pl.when(step > 0)
            def _():
                give_back(2, dv, dv_out, step - 1)

            return carry

        lax.fori_loop(0, genes, value_step, 0)
        arrived(vf, in_recv.at[3])
        give_back(2, dv, dv_out, genes - 1)

        def key_step(step, carry):
            _, _, j = peer(step)
            own = vf[block_of(j), :]
            total = jnp.zeros((BLOCK, BLOCK), F32)
            for n in range(genes * BLOCK // CHUNK):
                span = slice(n * CHUNK, (n + 1) * CHUNK)
                wg = nt_dot(own, gf[span, :])
                delta = jnp.concatenate(
                    [statf[n * (CHUNK // BLOCK) + b, 1:2, :] for b in range(CHUNK // BLOCK)], axis=1
                )
                ds = weights[block_of(j), span] * (wg - delta)
                colsum[pl.ds(j, 1), span] = jnp.sum(ds, axis=0, keepdims=True)
                low = ds.astype(BF16)
                grads[block_of(j), span] = low
                total = total + nn_dot(low, qf[span, :])
            dk[block_of(j), :] = (total * scale).astype(BF16)

            @pl.when(step > 0)
            def _():
                give_back(1, dk, dk_out, step - 1)

            return carry

        lax.fori_loop(0, genes, key_step, 0)
        for i in range(genes):
            sums = jnp.sum(colsum[:, i * BLOCK : (i + 1) * BLOCK], axis=1, keepdims=True)
            terms[i, 0:1, 0:genes] = jnp.sum(jnp.where(listed(i), sums, 0.0), axis=0, keepdims=True)
        give_back(1, dk, dk_out, genes - 1)

        def query_step(step, carry):
            _, _, i = peer(step)
            across = nn_dot(kt[...], grads[:, block_of(i)])
            dq[block_of(i), :] = (across.T * scale).astype(BF16)

            @pl.when(step > 0)
            def _():
                give_back(0, dq, dq_out, step - 1)

            @pl.when(step == 0)
            def _():
                for to_step in range(1, genes):
                    to = peer(to_step)[2]
                    pltpu.make_async_remote_copy(
                        src_ref=terms.at[to],
                        dst_ref=mine.at[head],
                        send_sem=term_send,
                        recv_sem=term_recv,
                        device_id={"gene": to},
                        device_id_type=MESH,
                    ).start()
                pltpu.make_async_copy(terms.at[gene], mine.at[head], term_recv).start()

            return carry

        lax.fori_loop(0, genes, query_step, 0)

    arrived(mine, term_recv)
    for h in range(heads):
        packed[h : h + 1, :] = mine[h, 0:1, :]

    @pl.when(active)
    def _():
        give_back(0, dq, dq_out, genes - 1)

    for step in range(1, cells):
        pltpu.make_async_remote_copy(
            src_ref=packed,
            dst_ref=everyones.at[cell],
            send_sem=cell_send,
            recv_sem=cell_recv,
            device_id={"cell": (cell + step) % cells},
            device_id_type=MESH,
        ).start()
    own_packed = pltpu.make_async_copy(packed, everyones.at[cell], cell_recv)
    own_packed.start()
    arrived(everyones, cell_recv)
    everything = jnp.sum(everyones[...], axis=0)
    slot_lanes = lax.broadcasted_iota(jnp.int32, everything.shape, 1)
    picked = jnp.sum(jnp.where(slot_lanes == cell, everything, 0.0), axis=1, keepdims=True)
    bias_out[0] = picked[0:heads, :]

    for a, out in enumerate((dq_out, dk_out, dv_out)):
        arrived(out, out_recv.at[a])

    def sent(ref, count, sem):
        part = ref.at[pl.ds(0, count)]
        pltpu.make_async_copy(part, part, sem).wait()

    @pl.when(active)
    def _():
        for a in range(4):
            sent(kf, (heads - 1) * BLOCK, in_send.at[a])
        sent(statf, heads - 1, in_send.at[4])
        for a in range(3):
            sent(dq, (genes - 1) * BLOCK, out_send.at[a])
        sent(terms, genes - 1, term_send)

    @pl.when(jnp.logical_not(active))
    def _():
        for a in range(4):
            sent(kf, heads * BLOCK, in_send.at[a])
        sent(statf, heads, in_send.at[4])

    if cells > 1:
        sent(everyones, cells - 1, cell_send)


def shards(
    query_rows,
    key_rows,
    value_rows,
    output_rows,
    output_grad,
    row_lse,
    block_bias,
    block_index,
    block_count,
):
    heads = row_lse.shape[2]
    genes = block_index.shape[0]
    cells = lax.axis_size("cell")
    rows = genes * BLOCK
    anywhere = pl.BlockSpec(memory_space=pl.ANY)
    vmem = pl.BlockSpec(memory_space=pltpu.VMEM)
    smem = pl.BlockSpec(memory_space=pltpu.SMEM)
    flat = jax.ShapeDtypeStruct(query_rows.shape, BF16)
    dma = pltpu.SemaphoreType.DMA
    return pl.pallas_call(
        functools.partial(kernel, heads, genes, cells),
        out_shape=(flat, flat, flat, jax.ShapeDtypeStruct((1, heads, 1), F32)),
        in_specs=[anywhere] * 5 + [vmem, vmem, vmem, smem],
        out_specs=(anywhere, anywhere, anywhere, vmem),
        scratch_shapes=[
            pltpu.VMEM((rows, BLOCK), BF16),
            pltpu.VMEM((rows, BLOCK), BF16),
            pltpu.VMEM((rows, BLOCK), BF16),
            pltpu.VMEM((rows, BLOCK), BF16),
            pltpu.VMEM((genes, 8, BLOCK), F32),
            pltpu.VMEM((BLOCK, heads * BLOCK), BF16),
            pltpu.VMEM((BLOCK, heads * BLOCK), BF16),
            pltpu.VMEM((heads, 8, BLOCK), F32),
            pltpu.VMEM((BLOCK, BLOCK), F32),
            pltpu.VMEM((BLOCK, rows), BF16),
            pltpu.VMEM((genes, rows), F32),
            pltpu.VMEM((rows, rows), F32),
            pltpu.VMEM((rows, rows), BF16),
            pltpu.VMEM((genes, rows), F32),
            pltpu.VMEM((rows, BLOCK), BF16),
            pltpu.VMEM((rows, BLOCK), BF16),
            pltpu.VMEM((rows, BLOCK), BF16),
            pltpu.VMEM((genes, 8, BLOCK), F32),
            pltpu.VMEM((heads, 8, BLOCK), F32),
            pltpu.VMEM((16, BLOCK), F32),
            pltpu.VMEM((cells, 16, BLOCK), F32),
            dma((2,)),
            dma((5,)),
            dma((5,)),
            dma((3,)),
            dma((3,)),
            dma,
            dma,
            dma,
            dma,
        ],
        compiler_params=pltpu.CompilerParams(
            collective_id=0, has_side_effects=True, vmem_limit_bytes=48 * 1024 * 1024
        ),
    )(
        query_rows,
        key_rows,
        value_rows,
        output_rows,
        output_grad,
        row_lse,
        block_bias,
        block_index,
        block_count,
    )


def solution(mesh):
    in_specs = (
        P("cell", "gene", None),
        P("cell", "gene", None),
        P("cell", "gene", None),
        P("cell", "gene", None),
        P("cell", "gene", None),
        P("cell", "gene", None),
        P(),
        P(),
        P(),
    )
    out_specs = (
        P("cell", "gene", None),
        P("cell", "gene", None),
        P("cell", "gene", None),
        P("gene", None, "cell"),
    )
    return jax.shard_map(shards, mesh=mesh, in_specs=in_specs, out_specs=out_specs, check_vma=False)
```

```python
import functools
import math

import jax
import jax.numpy as jnp
from jax import lax
from jax.experimental import pallas as pl
from jax.experimental.pallas import tpu as pltpu
from jax.sharding import PartitionSpec as P

MESH = pl.DeviceIdType.MESH
BLOCK = 128
SIDE = 4
WIDE = 256
TALL = 512
LOG2E = 1.4426950408889634
OFF = -1.0e30
BF16 = jnp.bfloat16
F32 = jnp.float32


def nt_dot(a, b):
    return lax.dot_general(a, b, (((1,), (1,)), ((), ())), preferred_element_type=F32)


def nn_dot(a, b):
    return jnp.dot(a, b, preferred_element_type=F32)


def kernel(
    heads,
    genes,
    cells,
    q_in,
    k_in,
    v_in,
    o_in,
    g_in,
    lse_in,
    bias_in,
    index_in,
    count_in,
    dq_out,
    dk_out,
    dv_out,
    bias_out,
    qf,
    kf,
    vf,
    gf,
    statf,
    o_own,
    g_own,
    stat,
    square,
    kt,
    addend,
    weights,
    low,
    colsum,
    dq,
    dk,
    dv,
    terms,
    mine,
    everyones,
    lse_own,
    bias_own,
    index_own,
    count_own,
    load_sem,
    in_send,
    in_recv,
    out_send,
    out_recv,
    term_send,
    term_recv,
    cell_send,
    cell_recv,
):
    gene = lax.axis_index("gene")
    cell = lax.axis_index("cell")
    row, col = gene // SIDE, gene % SIDE
    turn = 2 * (cell % 2) + (cell // 2) % 2
    live_heads = heads // SIDE
    scale = 1.0 / math.sqrt(BLOCK)

    def slot_of(r, c):
        return (r + turn) % SIDE

    place = slot_of(row, col)
    active = place < live_heads
    head = live_heads * col + place
    head_cols = pl.ds(pl.multiple_of(head * BLOCK, BLOCK), BLOCK)

    def peer(step):
        r, c = (row + step // SIDE) % SIDE, (col + step % SIDE) % SIDE
        return r, c, r * SIDE + c

    def block_of(i):
        return pl.ds(pl.multiple_of(i * BLOCK, BLOCK), BLOCK)

    barrier = pltpu.get_barrier_semaphore()
    for step in range(1, genes):
        pl.semaphore_signal(barrier, inc=1, device_id={"gene": peer(step)[2]}, device_id_type=MESH)
    for step in range(1, cells):
        pl.semaphore_signal(
            barrier, inc=1, device_id={"cell": (cell + step) % cells}, device_id_type=MESH
        )

    loads = [
        pltpu.make_async_copy(src, dst, load_sem.at[n])
        for n, (src, dst) in enumerate(
            (
                (o_in.at[0], o_own),
                (g_in.at[0], g_own),
                (lse_in, lse_own),
                (bias_in, bias_own),
                (index_in, index_own),
                (count_in, count_own),
            )
        )
    ]
    for load in loads:
        load.start()
    pl.semaphore_wait(barrier, genes + cells - 2)

    moved = ((k_in, kf), (q_in, qf), (g_in, gf), (v_in, vf))

    def send_array(a, src, dst):
        for step in range(1, genes):
            r, c, to = peer(step)
            spot = slot_of(r, c)

            @pl.when(spot < live_heads)
            def _():
                cols = pl.ds(pl.multiple_of((live_heads * c + spot) * BLOCK, BLOCK), BLOCK)
                pltpu.make_async_remote_copy(
                    src_ref=src.at[0, :, cols],
                    dst_ref=dst.at[block_of(gene), :],
                    send_sem=in_send.at[a],
                    recv_sem=in_recv.at[a],
                    device_id={"gene": to},
                    device_id_type=MESH,
                ).start()

        @pl.when(active)
        def _():
            pltpu.make_async_copy(
                src.at[0, :, head_cols], dst.at[block_of(gene), :], in_recv.at[a]
            ).start()

    send_array(0, *moved[0])
    send_array(1, *moved[1])
    terms[...] = jnp.zeros_like(terms)
    lanes = lax.broadcasted_iota(jnp.int32, (BLOCK, BLOCK), 1)
    for load in loads:
        load.wait()
    deltas = jnp.zeros((BLOCK, BLOCK), F32)
    for h in range(heads):
        cols = slice(h * BLOCK, (h + 1) * BLOCK)
        one = jnp.sum(
            g_own[:, cols].astype(F32) * o_own[:, cols].astype(F32), axis=1, keepdims=True
        )
        deltas = jnp.where(lanes == h, one, deltas)
    turned = deltas.T
    for h in range(heads):
        stat[h, 0:1, :] = lse_own[h]
        stat[h, 1:2, :] = turned[h : h + 1, :]

    for step in range(1, genes):
        r, c, to = peer(step)
        spot = slot_of(r, c)

        @pl.when(spot < live_heads)
        def _():
            pltpu.make_async_remote_copy(
                src_ref=stat.at[live_heads * c + spot],
                dst_ref=statf.at[gene],
                send_sem=in_send.at[4],
                recv_sem=in_recv.at[4],
                device_id={"gene": to},
                device_id_type=MESH,
            ).start()

    @pl.when(active)
    def _():
        pltpu.make_async_copy(stat.at[head], statf.at[gene], in_recv.at[4]).start()

    send_array(2, *moved[2])
    send_array(3, *moved[3])

    def arrived(ref, sem):
        pltpu.make_async_copy(ref, ref, sem).wait()

    def give_back(a, src, dst, to):
        @pl.when(to == gene)
        def _():
            pltpu.make_async_copy(
                src.at[block_of(to), :], dst.at[0, :, head_cols], out_recv.at[a]
            ).start()

        @pl.when(to != gene)
        def _():
            pltpu.make_async_remote_copy(
                src_ref=src.at[block_of(to), :],
                dst_ref=dst.at[0, :, head_cols],
                send_sem=out_send.at[a],
                recv_sem=out_recv.at[a],
                device_id={"gene": to},
                device_id_type=MESH,
            ).start()

    wides = genes * BLOCK // WIDE
    per_wide = WIDE // BLOCK

    def wide_at(step):
        return (gene // per_wide + step) % wides

    def wide_of(n):
        return pl.ds(pl.multiple_of(n * WIDE, WIDE), WIDE)

    def give_wide_back(a, src, dst, step):
        for b in range(per_wide):
            give_back(a, src, dst, wide_at(step) * per_wide + b)

    def over_queries(m, right):
        total = jnp.zeros((WIDE, BLOCK), F32)
        for n in range(wides):
            total = total + nn_dot(low[n, wide_of(m), :], right[n * WIDE : (n + 1) * WIDE, :])
        return total

    keys_iota = lax.broadcasted_iota(jnp.int32, (genes, genes), 0)
    slot_iota = lax.broadcasted_iota(jnp.int32, (genes, genes), 1)

    def listed(i):
        return (index_own[i : i + 1, :] == keys_iota) & (slot_iota < count_own[i])

    @pl.when(active)
    def _():
        arrived(statf, in_recv.at[4])
        for i in range(genes):
            hit = listed(i)
            bias_row = bias_own[head, i : i + 1, :]
            bias_col = jnp.sum(jnp.where(hit, bias_row, 0.0), axis=1, keepdims=True)
            hit_col = jnp.sum(jnp.where(hit, 1.0, 0.0), axis=1, keepdims=True)
            start = jnp.where(hit_col > 0.5, bias_col * LOG2E, OFF)
            n, at = i // per_wide, i % per_wide * BLOCK
            addend[n, :, at : at + BLOCK] = start - statf[i, 0:1, :] * LOG2E
        arrived(kf, in_recv.at[0])

        def turn_keys(i, carry):
            kt[:, block_of(i)] = kf[block_of(i), :].T
            return carry

        lax.fori_loop(0, genes, turn_keys, 0)
        arrived(qf, in_recv.at[1])

        def score_step(n, carry):
            own = qf[wide_of(n), :]
            for m in range(0, genes * BLOCK, TALL):
                scores = nt_dot(kf[m : m + TALL, :], own)
                for b in range(0, TALL, BLOCK):
                    j = (m + b) // BLOCK
                    span = slice(m + b, m + b + BLOCK)
                    w = jnp.exp2(
                        scores[b : b + BLOCK, :] * (scale * LOG2E) + addend[n, j : j + 1, :]
                    )
                    weights[n, span, :] = w
                    low[n, span, :] = w.astype(BF16)
            return carry

        lax.fori_loop(0, wides, score_step, 0)
        arrived(gf, in_recv.at[2])

        def value_step(step, carry):
            m = wide_at(step)
            dv[wide_of(m), :] = over_queries(m, gf).astype(BF16)

            @pl.when(step > 0)
            def _():
                give_wide_back(2, dv, dv_out, step - 1)

            return carry

        lax.fori_loop(0, wides, value_step, 0)
        arrived(vf, in_recv.at[3])
        give_wide_back(2, dv, dv_out, wides - 1)

        def grad_step(step, carry):
            n = wide_at(step)
            own = gf[wide_of(n), :]
            delta = jnp.concatenate(
                [statf[n * per_wide + b, 1:2, :] for b in range(per_wide)], axis=1
            )
            for m in range(0, genes * BLOCK, TALL):
                wg = nt_dot(vf[m : m + TALL, :], own)
                for b in range(0, TALL, BLOCK):
                    j = (m + b) // BLOCK
                    span = slice(m + b, m + b + BLOCK)
                    ds = weights[n, span, :] * (wg[b : b + BLOCK, :] - delta)
                    colsum[n, j : j + 1, :] = jnp.sum(ds, axis=0, keepdims=True)
                    low[n, span, :] = ds.astype(BF16)
            return carry

        lax.fori_loop(0, wides, grad_step, 0)
        for i in range(genes):
            n, at = i // per_wide, i % per_wide * BLOCK
            sums = jnp.sum(colsum[n, :, at : at + BLOCK], axis=1, keepdims=True)
            terms[i, :, 0:genes] = jnp.sum(jnp.where(listed(i), sums, 0.0), axis=0, keepdims=True)

        def query_step(step, carry):
            n = wide_at(step)
            across = nn_dot(kt[...], low[n])
            dq[wide_of(n), :] = (across.T * scale).astype(BF16)

            @pl.when(step > 0)
            def _():
                give_wide_back(0, dq, dq_out, step - 1)

            @pl.when(step == 0)
            def _():
                for to_step in range(1, genes):
                    to = peer(to_step)[2]
                    pltpu.make_async_remote_copy(
                        src_ref=terms.at[to],
                        dst_ref=mine.at[head],
                        send_sem=term_send,
                        recv_sem=term_recv,
                        device_id={"gene": to},
                        device_id_type=MESH,
                    ).start()
                pltpu.make_async_copy(terms.at[gene], mine.at[head], term_recv).start()

            return carry

        lax.fori_loop(0, wides, query_step, 0)
        give_wide_back(0, dq, dq_out, wides - 1)

        def key_step(step, carry):
            m = wide_at(step)
            dk[wide_of(m), :] = (over_queries(m, qf) * scale).astype(BF16)

            @pl.when(step > 0)
            def _():
                give_wide_back(1, dk, dk_out, step - 1)

            return carry

        lax.fori_loop(0, wides, key_step, 0)
        give_wide_back(1, dk, dk_out, wides - 1)

    square[...] = jnp.zeros_like(square)
    arrived(mine, term_recv)
    for step in range(1, cells):
        pltpu.make_async_remote_copy(
            src_ref=mine,
            dst_ref=everyones.at[cell],
            send_sem=cell_send,
            recv_sem=cell_recv,
            device_id={"cell": (cell + step) % cells},
            device_id_type=MESH,
        ).start()
    pltpu.make_async_copy(mine, everyones.at[cell], cell_recv).start()
    arrived(everyones, cell_recv)
    everything = jnp.sum(everyones[...], axis=0)
    for h in range(heads):
        square[h : h + 1, :] = everything[h]
    slot_rows = lax.broadcasted_iota(jnp.int32, (BLOCK, BLOCK), 0)
    picked = jnp.sum(jnp.where(slot_rows == cell, square[...].T, 0.0), axis=0, keepdims=True)
    bias_out[0] = picked[:, 0:heads]

    for a, out in enumerate((dq_out, dk_out, dv_out)):
        arrived(out, out_recv.at[a])

    def sent(ref, count, sem):
        part = ref.at[pl.ds(0, count)]
        pltpu.make_async_copy(part, part, sem).wait()

    @pl.when(active)
    def _():
        for a in range(4):
            sent(kf, (heads - 1) * BLOCK, in_send.at[a])
        sent(statf, heads - 1, in_send.at[4])
        for a in range(3):
            sent(dq, (genes - 1) * BLOCK, out_send.at[a])
        sent(terms, genes - 1, term_send)

    @pl.when(jnp.logical_not(active))
    def _():
        for a in range(4):
            sent(kf, heads * BLOCK, in_send.at[a])
        sent(statf, heads, in_send.at[4])

    if cells > 1:
        sent(everyones, cells - 1, cell_send)


def put_out(*refs):
    count = (len(refs) - 1) // 2
    copies = [
        pltpu.make_async_copy(refs[n], refs[count + n], refs[-1].at[n]) for n in range(count)
    ]
    for copy in copies:
        copy.start()
    for copy in copies:
        copy.wait()


def shards(
    query_rows,
    key_rows,
    value_rows,
    output_rows,
    output_grad,
    row_lse,
    block_bias,
    block_index,
    block_count,
):
    heads = row_lse.shape[2]
    genes = block_index.shape[0]
    cells = lax.axis_size("cell")
    rows = genes * BLOCK
    anywhere = pl.BlockSpec(memory_space=pl.ANY)
    vmem = pl.BlockSpec(memory_space=pltpu.VMEM)
    flat = jax.ShapeDtypeStruct(query_rows.shape, BF16)
    dma = pltpu.SemaphoreType.DMA
    wides = rows // WIDE
    held = pltpu.VMEM(query_rows.shape, BF16)
    bias_flat = (1, 1, heads)
    results = pl.pallas_call(
        functools.partial(kernel, heads, genes, cells),
        out_shape=(held, held, held, pltpu.VMEM(bias_flat, F32)),
        in_specs=[pl.BlockSpec(memory_space=pltpu.HBM)] * 9,
        out_specs=(vmem, vmem, vmem, vmem),
        scratch_shapes=[
            pltpu.VMEM((rows, BLOCK), BF16),
            pltpu.VMEM((rows, BLOCK), BF16),
            pltpu.VMEM((rows, BLOCK), BF16),
            pltpu.VMEM((rows, BLOCK), BF16),
            pltpu.VMEM((genes, 2, BLOCK), F32),
            pltpu.VMEM((BLOCK, heads * BLOCK), BF16),
            pltpu.VMEM((BLOCK, heads * BLOCK), BF16),
            pltpu.VMEM((heads, 2, BLOCK), F32),
            pltpu.VMEM((BLOCK, BLOCK), F32),
            pltpu.VMEM((BLOCK, rows), BF16),
            pltpu.VMEM((wides, genes, WIDE), F32),
            pltpu.VMEM((wides, rows, WIDE), F32),
            pltpu.VMEM((wides, rows, WIDE), BF16),
            pltpu.VMEM((wides, genes, WIDE), F32),
            pltpu.VMEM((rows, BLOCK), BF16),
            pltpu.VMEM((rows, BLOCK), BF16),
            pltpu.VMEM((rows, BLOCK), BF16),
            pltpu.VMEM((genes, 1, BLOCK), F32),
            pltpu.VMEM((heads, 1, BLOCK), F32),
            pltpu.VMEM((cells, heads, 1, BLOCK), F32),
            pltpu.VMEM((heads, 1, BLOCK), F32),
            pltpu.VMEM((heads, genes, genes), F32),
            pltpu.VMEM((genes, genes), jnp.int32),
            pltpu.SMEM((genes,), jnp.int32),
            dma((6,)),
            dma((5,)),
            dma((5,)),
            dma((3,)),
            dma((3,)),
            dma,
            dma,
            dma,
            dma,
        ],
        compiler_params=pltpu.CompilerParams(
            collective_id=0, has_side_effects=True, vmem_limit_bytes=60 * 1024 * 1024
        ),
    )(
        query_rows,
        key_rows,
        value_rows,
        output_rows,
        output_grad,
        jnp.transpose(row_lse, (2, 0, 1)),
        jnp.transpose(block_bias, (1, 0, 2)),
        block_index,
        block_count,
    )
    query_grad, key_grad, value_grad, bias_grad = pl.pallas_call(
        put_out,
        out_shape=(flat, flat, flat, jax.ShapeDtypeStruct(bias_flat, F32)),
        in_specs=[anywhere] * 4,
        out_specs=(anywhere,) * 4,
        scratch_shapes=[dma((4,))],
        compiler_params=pltpu.CompilerParams(vmem_limit_bytes=1024 * 1024),
    )(*(pltpu.with_memory_space_constraint(r, pltpu.VMEM) for r in results))
    return (query_grad, key_grad, value_grad, jnp.transpose(bias_grad, (0, 2, 1)))


def solution(mesh):
    in_specs = (
        P("cell", "gene", None),
        P("cell", "gene", None),
        P("cell", "gene", None),
        P("cell", "gene", None),
        P("cell", "gene", None),
        P("cell", "gene", None),
        P(),
        P(),
        P(),
    )
    out_specs = (
        P("cell", "gene", None),
        P("cell", "gene", None),
        P("cell", "gene", None),
        P("gene", None, "cell"),
    )
    return jax.shard_map(shards, mesh=mesh, in_specs=in_specs, out_specs=out_specs, check_vma=False)
```

```python
import functools
import math

import jax
import jax.numpy as jnp
from jax import lax
from jax.experimental import pallas as pl
from jax.experimental.pallas import tpu as pltpu
from jax.sharding import PartitionSpec as P

MESH = pl.DeviceIdType.MESH
BLOCK = 128
SIDE = 4
WIDE = 256
TALL = 512
UNROLL = 4
LOG2E = 1.4426950408889634
OFF = -1.0e30
BF16 = jnp.bfloat16
F32 = jnp.float32


def nt_dot(a, b):
    return lax.dot_general(a, b, (((1,), (1,)), ((), ())), preferred_element_type=F32)


def nn_dot(a, b):
    return jnp.dot(a, b, preferred_element_type=F32)


def kernel(
    heads,
    genes,
    cells,
    q_in,
    k_in,
    v_in,
    o_in,
    g_in,
    lse_in,
    bias_in,
    index_in,
    count_in,
    dq_out,
    dk_out,
    dv_out,
    bias_out,
    qf,
    kf,
    vf,
    gf,
    statf,
    o_own,
    g_own,
    stat,
    square,
    kt,
    addend,
    weights,
    low,
    colsum,
    dq,
    dk,
    dv,
    terms,
    mine,
    everyones,
    relay,
    lse_own,
    bias_own,
    index_own,
    count_own,
    load_sem,
    in_send,
    in_recv,
    v_recv,
    out_send,
    out_recv,
    relay_recv,
    term_send,
    term_recv,
    cell_send,
    cell_recv,
):
    gene = lax.axis_index("gene")
    cell = lax.axis_index("cell")
    row, col = gene // SIDE, gene % SIDE
    core, half = cell % 2, (cell // 2) % 2
    other = cell + 2 - 4 * half
    live_heads = heads // SIDE
    scale = 1.0 / math.sqrt(BLOCK)

    def slot_of(r, side):
        return (r + 2 * core + side) % SIDE

    def device_at(to):
        return {"cell": other, "gene": to}

    place = slot_of(row, half)
    active = place < live_heads
    head = live_heads * col + place
    head_cols = pl.ds(pl.multiple_of(head * BLOCK, BLOCK), BLOCK)

    beside_row = row + 1 - 2 * (row % 2)
    beside = beside_row * SIDE + col
    beside_place = slot_of(beside_row, half)
    helped = jnp.logical_and(active, beside_place >= live_heads)
    beside_cols = pl.ds(
        pl.multiple_of((live_heads * col + beside_place) * BLOCK, BLOCK), BLOCK
    )
    way = 2 * half - 1
    near = 2 * SIDE

    def peer(step):
        r, c = (row + step // SIDE) % SIDE, (col + step % SIDE) % SIDE
        return r, c, r * SIDE + c

    def block_of(i):
        return pl.ds(pl.multiple_of(i * BLOCK, BLOCK), BLOCK)

    barrier = pltpu.get_barrier_semaphore()
    for step in range(genes):
        pl.semaphore_signal(barrier, inc=1, device_id=device_at(peer(step)[2]), device_id_type=MESH)
    pl.semaphore_signal(barrier, inc=1, device_id={"gene": beside}, device_id_type=MESH)
    for step in range(1, cells):
        pl.semaphore_signal(
            barrier, inc=1, device_id={"cell": (cell + step) % cells}, device_id_type=MESH
        )

    loads = [
        pltpu.make_async_copy(src, dst, load_sem.at[n])
        for n, (src, dst) in enumerate(
            (
                (o_in.at[0], o_own),
                (g_in.at[0], g_own),
                (lse_in, lse_own),
                (bias_in, bias_own),
                (index_in, index_own),
                (count_in, count_own),
            )
        )
    ]
    for load in loads:
        load.start()
    pl.semaphore_wait(barrier, genes + cells)

    moved = ((k_in, kf), (q_in, qf), (g_in, gf), (v_in, vf))

    def send_array(a, src, dst, recv_sem):
        for step in range(genes):
            r, c, to = peer(step)
            spot = slot_of(r, 1 - half)

            @pl.when(spot < live_heads)
            def _():
                cols = pl.ds(pl.multiple_of((live_heads * c + spot) * BLOCK, BLOCK), BLOCK)
                pltpu.make_async_remote_copy(
                    src_ref=src.at[0, :, cols],
                    dst_ref=dst.at[block_of(gene), :],
                    send_sem=in_send.at[a],
                    recv_sem=recv_sem,
                    device_id=device_at(to),
                    device_id_type=MESH,
                ).start()

    send_array(0, *moved[0], in_recv.at[0])
    send_array(1, *moved[1], in_recv.at[1])
    terms[...] = jnp.zeros_like(terms)
    lanes = lax.broadcasted_iota(jnp.int32, (BLOCK, BLOCK), 1)
    for load in loads:
        load.wait()
    deltas = jnp.zeros((BLOCK, BLOCK), F32)
    for h in range(heads):
        cols = slice(h * BLOCK, (h + 1) * BLOCK)
        one = jnp.sum(
            g_own[:, cols].astype(F32) * o_own[:, cols].astype(F32), axis=1, keepdims=True
        )
        deltas = jnp.where(lanes == h, one, deltas)
    turned = deltas.T
    for h in range(heads):
        stat[h, 0:1, :] = lse_own[h]
        stat[h, 1:2, :] = turned[h : h + 1, :]

    for step in range(genes):
        r, c, to = peer(step)
        spot = slot_of(r, 1 - half)

        @pl.when(spot < live_heads)
        def _():
            pltpu.make_async_remote_copy(
                src_ref=stat.at[live_heads * c + spot],
                dst_ref=statf.at[gene],
                send_sem=in_send.at[4],
                recv_sem=in_recv.at[4],
                device_id=device_at(to),
                device_id_type=MESH,
            ).start()

    send_array(2, *moved[2], in_recv.at[2])
    send_array(3, *moved[3], v_recv.at[row])

    def arrived(ref, sem):
        pltpu.make_async_copy(ref, ref, sem).wait()

    def give_direct(a, src, dst, to):
        pltpu.make_async_remote_copy(
            src_ref=src.at[block_of(to), :],
            dst_ref=dst.at[0, :, head_cols],
            send_sem=out_send.at[a],
            recv_sem=out_recv.at[a],
            device_id=device_at(to),
            device_id_type=MESH,
        ).start()

    def place_near(to):
        return ((to % SIDE - col) * way + 2 * SIDE) % SIDE * SIDE + to // SIDE

    def give_relay(a, src, to):
        pltpu.make_async_remote_copy(
            src_ref=src.at[block_of(to), :],
            dst_ref=relay.at[a, block_of(place_near(to)), :],
            send_sem=out_send.at[a],
            recv_sem=relay_recv.at[a],
            device_id={"gene": beside},
            device_id_type=MESH,
        ).start()

    def near_gene(k):
        return k % SIDE * SIDE + (col + k // SIDE * way + SIDE) % SIDE

    def give_back(a, src, dst, to):
        by_relay = jnp.logical_and(helped, place_near(to) < near)

        @pl.when(by_relay)
        def _():
            give_relay(a, src, to)

        @pl.when(jnp.logical_not(by_relay))
        def _():
            give_direct(a, src, dst, to)

    def pass_on(a, dst):
        arrived(relay.at[a], relay_recv.at[a])
        for k in range(near):
            pltpu.make_async_remote_copy(
                src_ref=relay.at[a, block_of(k), :],
                dst_ref=dst.at[0, :, beside_cols],
                send_sem=out_send.at[a],
                recv_sem=out_recv.at[a],
                device_id=device_at(near_gene(k)),
                device_id_type=MESH,
            ).start()

    wides = genes * BLOCK // WIDE
    per_wide = WIDE // BLOCK

    def wide_at(step):
        return (gene // per_wide + step) % wides

    def wide_of(n):
        return pl.ds(pl.multiple_of(n * WIDE, WIDE), WIDE)

    def give_wide_back(a, src, dst, step):
        for b in range(per_wide):
            give_back(a, src, dst, wide_at(step) * per_wide + b)

    def over_queries(m, right):
        total = jnp.zeros((WIDE, BLOCK), F32)
        for n in range(wides):
            total = total + nn_dot(low[n, wide_of(m), :], right[n * WIDE : (n + 1) * WIDE, :])
        return total

    keys_iota = lax.broadcasted_iota(jnp.int32, (genes, genes), 0)
    slot_iota = lax.broadcasted_iota(jnp.int32, (genes, genes), 1)

    def listed(i):
        return (index_own[i : i + 1, :] == keys_iota) & (slot_iota < count_own[i])

    @pl.when(active)
    def _():
        arrived(statf, in_recv.at[4])
        for i in range(genes):
            hit = listed(i)
            bias_row = bias_own[head, i : i + 1, :]
            bias_col = jnp.sum(jnp.where(hit, bias_row, 0.0), axis=1, keepdims=True)
            hit_col = jnp.sum(jnp.where(hit, 1.0, 0.0), axis=1, keepdims=True)
            start = jnp.where(hit_col > 0.5, bias_col * LOG2E, OFF)
            n, at = i // per_wide, i % per_wide * BLOCK
            addend[n, :, at : at + BLOCK] = start - statf[i, 0:1, :] * LOG2E
        arrived(kf, in_recv.at[0])

        def turn_keys(i, carry):
            kt[:, block_of(i)] = kf[block_of(i), :].T
            return carry

        lax.fori_loop(0, genes, turn_keys, 0)
        arrived(qf, in_recv.at[1])

        def score_step(n, carry):
            own = qf[wide_of(n), :]
            for m in range(0, genes * BLOCK, TALL):
                scores = nt_dot(kf[m : m + TALL, :], own)
                for b in range(0, TALL, BLOCK):
                    j = (m + b) // BLOCK
                    span = slice(m + b, m + b + BLOCK)
                    w = jnp.exp2(
                        scores[b : b + BLOCK, :] * (scale * LOG2E) + addend[n, j : j + 1, :]
                    )
                    weights[n, span, :] = w
                    low[n, span, :] = w.astype(BF16)
            return carry

        lax.fori_loop(0, wides, score_step, 0)
        arrived(gf, in_recv.at[2])

        def value_step(step, carry):
            m = wide_at(step)
            dv[wide_of(m), :] = over_queries(m, gf).astype(BF16)

            @pl.when(step > 0)
            def _():
                give_wide_back(2, dv, dv_out, step - 1)

            return carry

        lax.fori_loop(0, wides, value_step, 0)
        give_wide_back(2, dv, dv_out, wides - 1)

        def part_step(k, carry):
            part = (row + SIDE - k) % SIDE
            keys = pl.ds(pl.multiple_of(part * TALL, TALL), TALL)
            arrived(vf.at[keys, :], v_recv.at[part])

            def grad_step(lap, inner):
                for n in [lap * UNROLL + u for u in range(UNROLL)]:
                    delta = jnp.concatenate(
                        [statf[n * per_wide + b, 1:2, :] for b in range(per_wide)], axis=1
                    )
                    wg = nt_dot(vf[keys, :], gf[wide_of(n), :])
                    for b in range(TALL // BLOCK):
                        j = part * (TALL // BLOCK) + b
                        ds = weights[n, block_of(j), :] * (
                            wg[b * BLOCK : (b + 1) * BLOCK, :] - delta
                        )
                        colsum[n, pl.ds(j, 1), :] = jnp.sum(ds, axis=0, keepdims=True)
                        low[n, block_of(j), :] = ds.astype(BF16)
                return inner

            return lax.fori_loop(0, wides // UNROLL, grad_step, carry)

        lax.fori_loop(0, SIDE, part_step, 0)
        for i in range(genes):
            n, at = i // per_wide, i % per_wide * BLOCK
            sums = jnp.sum(colsum[n, :, at : at + BLOCK], axis=1, keepdims=True)
            terms[i, :, 0:genes] = jnp.sum(jnp.where(listed(i), sums, 0.0), axis=0, keepdims=True)

        def query_step(step, carry):
            n = wide_at(step)
            across = nn_dot(kt[...], low[n])
            dq[wide_of(n), :] = (across.T * scale).astype(BF16)

            @pl.when(step > 0)
            def _():
                give_wide_back(0, dq, dq_out, step - 1)

            @pl.when(step == 0)
            def _():
                for to_step in range(genes):
                    to = peer(to_step)[2]
                    pltpu.make_async_remote_copy(
                        src_ref=terms.at[to],
                        dst_ref=mine.at[head],
                        send_sem=term_send,
                        recv_sem=term_recv,
                        device_id=device_at(to),
                        device_id_type=MESH,
                    ).start()

            return carry

        lax.fori_loop(0, wides, query_step, 0)
        give_wide_back(0, dq, dq_out, wides - 1)

        def key_step(step, carry):
            m = wide_at(step)
            dk[wide_of(m), :] = (over_queries(m, qf) * scale).astype(BF16)
            return carry

        lax.fori_loop(0, wides, key_step, 0)
    @pl.when(jnp.logical_not(active))
    def _():
        pass_on(2, dv_out)
        pass_on(0, dq_out)

    square[...] = jnp.zeros_like(square)
    arrived(mine, term_recv)
    for step in range(1, cells):
        pltpu.make_async_remote_copy(
            src_ref=mine,
            dst_ref=everyones.at[cell],
            send_sem=cell_send,
            recv_sem=cell_recv,
            device_id={"cell": (cell + step) % cells},
            device_id_type=MESH,
        ).start()
    pltpu.make_async_copy(mine, everyones.at[cell], cell_recv).start()

    @pl.when(helped)
    def _():
        for k in range(near):
            give_relay(1, dk, near_gene(k))

    @pl.when(active)
    def _():
        for to in (0, 3, 4, 12, 1, 7, 8, 15, 2, 5, 11, 13, 6, 9, 14, 10):
            direct = jnp.logical_not(jnp.logical_and(helped, place_near(to) < near))

            @pl.when(direct)
            def _():
                give_direct(1, dk, dk_out, to)

    @pl.when(jnp.logical_not(active))
    def _():
        pass_on(1, dk_out)

    arrived(everyones, cell_recv)
    everything = jnp.sum(everyones[...], axis=0)
    for h in range(heads):
        square[h : h + 1, :] = everything[h]
    slot_rows = lax.broadcasted_iota(jnp.int32, (BLOCK, BLOCK), 0)
    picked = jnp.sum(jnp.where(slot_rows == cell, square[...].T, 0.0), axis=0, keepdims=True)
    bias_out[0] = picked[:, 0:heads]

    for a, out in enumerate((dq_out, dk_out, dv_out)):
        arrived(out, out_recv.at[a])

    def sent(ref, count, sem):
        part = ref.at[pl.ds(0, count)]
        pltpu.make_async_copy(part, part, sem).wait()

    for a in range(4):
        sent(kf, heads * BLOCK, in_send.at[a])
    sent(statf, heads, in_send.at[4])

    @pl.when(active)
    def _():
        for a in range(3):
            sent(dq, genes * BLOCK, out_send.at[a])
        sent(terms, genes, term_send)

    @pl.when(jnp.logical_not(active))
    def _():
        for a in range(3):
            sent(dq, near * BLOCK, out_send.at[a])

    if cells > 1:
        sent(everyones, cells - 1, cell_send)


def put_out(*refs):
    count = (len(refs) - 1) // 2
    copies = [
        pltpu.make_async_copy(refs[n], refs[count + n], refs[-1].at[n]) for n in range(count)
    ]
    for copy in copies:
        copy.start()
    for copy in copies:
        copy.wait()


def shards(
    query_rows,
    key_rows,
    value_rows,
    output_rows,
    output_grad,
    row_lse,
    block_bias,
    block_index,
    block_count,
):
    heads = row_lse.shape[2]
    genes = block_index.shape[0]
    cells = lax.axis_size("cell")
    rows = genes * BLOCK
    anywhere = pl.BlockSpec(memory_space=pl.ANY)
    vmem = pl.BlockSpec(memory_space=pltpu.VMEM)
    flat = jax.ShapeDtypeStruct(query_rows.shape, BF16)
    dma = pltpu.SemaphoreType.DMA
    wides = rows // WIDE
    held = pltpu.VMEM(query_rows.shape, BF16)
    bias_flat = (1, 1, heads)
    results = pl.pallas_call(
        functools.partial(kernel, heads, genes, cells),
        out_shape=(held, held, held, pltpu.VMEM(bias_flat, F32)),
        in_specs=[pl.BlockSpec(memory_space=pltpu.HBM)] * 9,
        out_specs=(vmem, vmem, vmem, vmem),
        scratch_shapes=[
            pltpu.VMEM((rows, BLOCK), BF16),
            pltpu.VMEM((rows, BLOCK), BF16),
            pltpu.VMEM((rows, BLOCK), BF16),
            pltpu.VMEM((rows, BLOCK), BF16),
            pltpu.VMEM((genes, 2, BLOCK), F32),
            pltpu.VMEM((BLOCK, heads * BLOCK), BF16),
            pltpu.VMEM((BLOCK, heads * BLOCK), BF16),
            pltpu.VMEM((heads, 2, BLOCK), F32),
            pltpu.VMEM((BLOCK, BLOCK), F32),
            pltpu.VMEM((BLOCK, rows), BF16),
            pltpu.VMEM((wides, genes, WIDE), F32),
            pltpu.VMEM((wides, rows, WIDE), F32),
            pltpu.VMEM((wides, rows, WIDE), BF16),
            pltpu.VMEM((wides, genes, WIDE), F32),
            pltpu.VMEM((rows, BLOCK), BF16),
            pltpu.VMEM((rows, BLOCK), BF16),
            pltpu.VMEM((rows, BLOCK), BF16),
            pltpu.VMEM((genes, 1, BLOCK), F32),
            pltpu.VMEM((heads, 1, BLOCK), F32),
            pltpu.VMEM((cells, heads, 1, BLOCK), F32),
            pltpu.VMEM((3, 2 * SIDE * BLOCK, BLOCK), BF16),
            pltpu.VMEM((heads, 1, BLOCK), F32),
            pltpu.VMEM((heads, genes, genes), F32),
            pltpu.VMEM((genes, genes), jnp.int32),
            pltpu.SMEM((genes,), jnp.int32),
            dma((6,)),
            dma((5,)),
            dma((5,)),
            dma((SIDE,)),
            dma((3,)),
            dma((3,)),
            dma((3,)),
            dma,
            dma,
            dma,
            dma,
        ],
        compiler_params=pltpu.CompilerParams(
            collective_id=0, has_side_effects=True, vmem_limit_bytes=60 * 1024 * 1024
        ),
    )(
        query_rows,
        key_rows,
        value_rows,
        output_rows,
        output_grad,
        jnp.transpose(row_lse, (2, 0, 1)),
        jnp.transpose(block_bias, (1, 0, 2)),
        block_index,
        block_count,
    )
    query_grad, key_grad, value_grad, bias_grad = pl.pallas_call(
        put_out,
        out_shape=(flat, flat, flat, jax.ShapeDtypeStruct(bias_flat, F32)),
        in_specs=[anywhere] * 4,
        out_specs=(anywhere,) * 4,
        scratch_shapes=[dma((4,))],
        compiler_params=pltpu.CompilerParams(vmem_limit_bytes=1024 * 1024),
    )(*(pltpu.with_memory_space_constraint(r, pltpu.VMEM) for r in results))
    return (query_grad, key_grad, value_grad, jnp.transpose(bias_grad, (0, 2, 1)))


def solution(mesh):
    in_specs = (
        P("cell", "gene", None),
        P("cell", "gene", None),
        P("cell", "gene", None),
        P("cell", "gene", None),
        P("cell", "gene", None),
        P("cell", "gene", None),
        P(),
        P(),
        P(),
    )
    out_specs = (
        P("cell", "gene", None),
        P("cell", "gene", None),
        P("cell", "gene", None),
        P("gene", None, "cell"),
    )
    return jax.shard_map(shards, mesh=mesh, in_specs=in_specs, out_specs=out_specs, check_vma=False)
```

```python
import functools
import math

import jax
import jax.numpy as jnp
from jax import lax
from jax.experimental import pallas as pl
from jax.experimental.pallas import tpu as pltpu
from jax.sharding import PartitionSpec as P

MESH = pl.DeviceIdType.MESH
BLOCK = 128
SIDE = 4
WIDE = 256
TALL = 512
UNROLL = 4
RELAYED = 8
LOG2E = 1.4426950408889634
OFF = -1.0e30
BF16 = jnp.bfloat16
F32 = jnp.float32


def nt_dot(a, b):
    return lax.dot_general(a, b, (((1,), (1,)), ((), ())), preferred_element_type=F32)


def nn_dot(a, b):
    return jnp.dot(a, b, preferred_element_type=F32)


def kernel(
    heads,
    genes,
    cells,
    q_in,
    k_in,
    v_in,
    o_in,
    g_in,
    lse_in,
    bias_in,
    index_in,
    count_in,
    dq_out,
    dk_out,
    dv_out,
    bias_out,
    qf,
    kf,
    vf,
    gf,
    statf,
    o_own,
    g_own,
    stat,
    square,
    kt,
    addend,
    weights,
    low,
    colsum,
    dq,
    dk,
    dv,
    terms,
    mine,
    everyones,
    relay,
    lse_own,
    bias_own,
    index_own,
    count_own,
    load_sem,
    in_send,
    in_recv,
    v_recv,
    out_send,
    out_recv,
    relay_recv,
    term_send,
    term_recv,
    cell_send,
    cell_recv,
):
    gene = lax.axis_index("gene")
    cell = lax.axis_index("cell")
    row, col = gene // SIDE, gene % SIDE
    core, half = cell % 2, (cell // 2) % 2
    other = cell + 2 - 4 * half
    live_heads = heads // SIDE
    scale = 1.0 / math.sqrt(BLOCK)

    def slot_of(r, side):
        return (r + 2 * core + side) % SIDE

    def device_at(to):
        return {"cell": other, "gene": to}

    place = slot_of(row, half)
    active = place < live_heads
    head = live_heads * col + place
    head_cols = pl.ds(pl.multiple_of(head * BLOCK, BLOCK), BLOCK)

    beside_row = row + 1 - 2 * (row % 2)
    beside = beside_row * SIDE + col
    beside_place = slot_of(beside_row, half)
    helped = jnp.logical_and(active, beside_place >= live_heads)
    beside_cols = pl.ds(
        pl.multiple_of((live_heads * col + beside_place) * BLOCK, BLOCK), BLOCK
    )

    def peer(step):
        r, c = (row + step // SIDE) % SIDE, (col + step % SIDE) % SIDE
        return r, c, r * SIDE + c

    def block_of(i):
        return pl.ds(pl.multiple_of(i * BLOCK, BLOCK), BLOCK)

    barrier = pltpu.get_barrier_semaphore()
    def alike(step):
        return (cell // 4 + step // 2) % (cells // 4) * 4 + 2 * half + (core + step) % 2

    for step in range(genes):
        to = peer(step)[2]
        pl.semaphore_signal(barrier, inc=1, device_id=device_at(to), device_id_type=MESH)
        if step > 0:
            pl.semaphore_signal(barrier, inc=1, device_id={"gene": to}, device_id_type=MESH)
    for step in range(1, cells // 2):
        pl.semaphore_signal(barrier, inc=1, device_id={"cell": alike(step)}, device_id_type=MESH)

    loads = [
        pltpu.make_async_copy(src, dst, load_sem.at[n])
        for n, (src, dst) in enumerate(
            (
                (o_in.at[0], o_own),
                (g_in.at[0], g_own),
                (lse_in, lse_own),
                (bias_in, bias_own),
                (index_in, index_own),
                (count_in, count_own),
            )
        )
    ]
    for load in loads:
        load.start()
    pl.semaphore_wait(barrier, 2 * genes + cells // 2 - 2)

    moved = ((k_in, kf), (q_in, qf), (g_in, gf), (v_in, vf))

    def send_array(a, src, dst, recv_sem):
        for step in range(genes):
            r, c, to = peer(step)
            spot = slot_of(r, 1 - half)

            @pl.when(spot < live_heads)
            def _():
                cols = pl.ds(pl.multiple_of((live_heads * c + spot) * BLOCK, BLOCK), BLOCK)
                pltpu.make_async_remote_copy(
                    src_ref=src.at[0, :, cols],
                    dst_ref=dst.at[block_of(gene), :],
                    send_sem=in_send.at[a],
                    recv_sem=recv_sem,
                    device_id=device_at(to),
                    device_id_type=MESH,
                ).start()

    send_array(0, *moved[0], in_recv.at[0])
    send_array(1, *moved[1], in_recv.at[1])
    terms[...] = jnp.zeros_like(terms)
    lanes = lax.broadcasted_iota(jnp.int32, (BLOCK, BLOCK), 1)
    for load in loads:
        load.wait()
    deltas = jnp.zeros((BLOCK, BLOCK), F32)
    for h in range(heads):
        cols = slice(h * BLOCK, (h + 1) * BLOCK)
        one = jnp.sum(
            g_own[:, cols].astype(F32) * o_own[:, cols].astype(F32), axis=1, keepdims=True
        )
        deltas = jnp.where(lanes == h, one, deltas)
    turned = deltas.T
    for h in range(heads):
        stat[h, 0:1, :] = lse_own[h]
        stat[h, 1:2, :] = turned[h : h + 1, :]

    for step in range(genes):
        r, c, to = peer(step)
        spot = slot_of(r, 1 - half)

        @pl.when(spot < live_heads)
        def _():
            pltpu.make_async_remote_copy(
                src_ref=stat.at[live_heads * c + spot],
                dst_ref=statf.at[gene],
                send_sem=in_send.at[4],
                recv_sem=in_recv.at[4],
                device_id=device_at(to),
                device_id_type=MESH,
            ).start()

    send_array(2, *moved[2], in_recv.at[2])
    send_array(3, *moved[3], v_recv.at[row])

    def arrived(ref, sem):
        pltpu.make_async_copy(ref, ref, sem).wait()

    def give_direct(a, src, dst, to):
        pltpu.make_async_remote_copy(
            src_ref=src.at[block_of(to), :],
            dst_ref=dst.at[0, :, head_cols],
            send_sem=out_send.at[a],
            recv_sem=out_recv.at[a],
            device_id=device_at(to),
            device_id_type=MESH,
        ).start()

    wides = genes * BLOCK // WIDE
    per_wide = WIDE // BLOCK

    def wide_at(step):
        return (gene // per_wide + step) % wides

    def wide_of(n):
        return pl.ds(pl.multiple_of(n * WIDE, WIDE), WIDE)

    lap = RELAYED // per_wide

    def give_wide_back(a, src, dst, step, relayed, stage):
        for b in range(per_wide):
            to = wide_at(step) * per_wide + b
            by_relay = jnp.logical_and(helped, step < relayed)

            @pl.when(by_relay)
            def _():
                pltpu.make_async_remote_copy(
                    src_ref=src.at[block_of(to), :],
                    dst_ref=relay.at[stage + step // lap, block_of(step % lap * per_wide + b), :],
                    send_sem=out_send.at[a],
                    recv_sem=relay_recv.at[stage + step // lap],
                    device_id={"gene": beside},
                    device_id_type=MESH,
                ).start()

            @pl.when(jnp.logical_not(by_relay))
            def _():
                give_direct(a, src, dst, to)

    def pass_on(a, dst, stage, first):
        arrived(relay.at[stage], relay_recv.at[stage])
        for k in range(RELAYED):
            m = (beside // per_wide + first + k // per_wide) % wides
            pltpu.make_async_remote_copy(
                src_ref=relay.at[stage, block_of(k), :],
                dst_ref=dst.at[0, :, beside_cols],
                send_sem=out_send.at[a],
                recv_sem=out_recv.at[a],
                device_id=device_at(m * per_wide + k % per_wide),
                device_id_type=MESH,
            ).start()

    def over_queries(m, right):
        total = jnp.zeros((WIDE, BLOCK), F32)
        for n in range(wides):
            total = total + nn_dot(low[n, wide_of(m), :], right[n * WIDE : (n + 1) * WIDE, :])
        return total

    keys_iota = lax.broadcasted_iota(jnp.int32, (genes, genes), 0)
    slot_iota = lax.broadcasted_iota(jnp.int32, (genes, genes), 1)

    def listed(i):
        return (index_own[i : i + 1, :] == keys_iota) & (slot_iota < count_own[i])

    @pl.when(active)
    def _():
        arrived(statf, in_recv.at[4])
        for i in range(genes):
            hit = listed(i)
            bias_row = bias_own[head, i : i + 1, :]
            bias_col = jnp.sum(jnp.where(hit, bias_row, 0.0), axis=1, keepdims=True)
            hit_col = jnp.sum(jnp.where(hit, 1.0, 0.0), axis=1, keepdims=True)
            start = jnp.where(hit_col > 0.5, bias_col * LOG2E, OFF)
            n, at = i // per_wide, i % per_wide * BLOCK
            addend[n, :, at : at + BLOCK] = start - statf[i, 0:1, :] * LOG2E
        arrived(kf, in_recv.at[0])

        def turn_keys(i, carry):
            kt[:, block_of(i)] = kf[block_of(i), :].T
            return carry

        lax.fori_loop(0, genes, turn_keys, 0)
        arrived(qf, in_recv.at[1])

        def score_step(n, carry):
            own = qf[wide_of(n), :]
            for m in range(0, genes * BLOCK, TALL):
                scores = nt_dot(kf[m : m + TALL, :], own)
                for b in range(0, TALL, BLOCK):
                    j = (m + b) // BLOCK
                    span = slice(m + b, m + b + BLOCK)
                    w = jnp.exp2(
                        scores[b : b + BLOCK, :] * (scale * LOG2E) + addend[n, j : j + 1, :]
                    )
                    weights[n, span, :] = w
                    low[n, span, :] = w.astype(BF16)
            return carry

        lax.fori_loop(0, wides, score_step, 0)
        arrived(gf, in_recv.at[2])

        def value_step(step, carry):
            m = wide_at(step)
            dv[wide_of(m), :] = over_queries(m, gf).astype(BF16)

            @pl.when(step > 0)
            def _():
                give_wide_back(2, dv, dv_out, step - 1, wides, 0)

            return carry

        lax.fori_loop(0, wides, value_step, 0)
        give_wide_back(2, dv, dv_out, wides - 1, wides, 0)

        def part_step(k, carry):
            part = (row + SIDE - k) % SIDE
            keys = pl.ds(pl.multiple_of(part * TALL, TALL), TALL)
            arrived(vf.at[keys, :], v_recv.at[part])

            def grad_step(lap, inner):
                for n in [lap * UNROLL + u for u in range(UNROLL)]:
                    delta = jnp.concatenate(
                        [statf[n * per_wide + b, 1:2, :] for b in range(per_wide)], axis=1
                    )
                    wg = nt_dot(vf[keys, :], gf[wide_of(n), :])
                    for b in range(TALL // BLOCK):
                        j = part * (TALL // BLOCK) + b
                        ds = weights[n, block_of(j), :] * (
                            wg[b * BLOCK : (b + 1) * BLOCK, :] - delta
                        )
                        colsum[n, pl.ds(j, 1), :] = jnp.sum(ds, axis=0, keepdims=True)
                        low[n, block_of(j), :] = ds.astype(BF16)
                return inner

            return lax.fori_loop(0, wides // UNROLL, grad_step, carry)

        lax.fori_loop(0, SIDE, part_step, 0)
        for i in range(genes):
            n, at = i // per_wide, i % per_wide * BLOCK
            sums = jnp.sum(colsum[n, :, at : at + BLOCK], axis=1, keepdims=True)
            terms[i, :, 0:genes] = jnp.sum(jnp.where(listed(i), sums, 0.0), axis=0, keepdims=True)

        def query_step(step, carry):
            n = wide_at(step)
            across = nn_dot(kt[...], low[n])
            dq[wide_of(n), :] = (across.T * scale).astype(BF16)

            @pl.when(step > 0)
            def _():
                give_wide_back(0, dq, dq_out, step - 1, lap, 2)

            @pl.when(step == 0)
            def _():
                for to_step in range(genes):
                    to = peer(to_step)[2]
                    pltpu.make_async_remote_copy(
                        src_ref=terms.at[to],
                        dst_ref=mine.at[1 - half, head],
                        send_sem=term_send.at[0],
                        recv_sem=term_recv,
                        device_id=device_at(to),
                        device_id_type=MESH,
                    ).start()
                    if to_step > 0:
                        pltpu.make_async_remote_copy(
                            src_ref=terms.at[to],
                            dst_ref=mine.at[1 - half, head],
                            send_sem=term_send.at[1],
                            recv_sem=term_recv,
                            device_id={"gene": to},
                            device_id_type=MESH,
                        ).start()
                pltpu.make_async_copy(terms.at[gene], mine.at[1 - half, head], term_recv).start()

            return carry

        lax.fori_loop(0, wides, query_step, 0)
        give_wide_back(0, dq, dq_out, wides - 1, lap, 2)

        def key_step(step, carry):
            m = wide_at(step)
            dk[wide_of(m), :] = (over_queries(m, qf) * scale).astype(BF16)
            return carry

        lax.fori_loop(0, wides, key_step, 0)
    @pl.when(active)
    def _():
        for to in (0, 3, 4, 12, 1, 7, 8, 15, 2, 5, 11, 13, 6, 9, 14, 10):
            give_direct(1, dk, dk_out, to)

    @pl.when(jnp.logical_not(active))
    def _():
        pass_on(2, dv_out, 0, 0)
        pass_on(2, dv_out, 1, lap)
        pass_on(0, dq_out, 2, 0)

    square[...] = jnp.zeros_like(square)
    arrived(mine, term_recv)
    own_place = cell // 4 * 2 + core
    for step in range(1, cells // 2):
        pltpu.make_async_remote_copy(
            src_ref=mine,
            dst_ref=everyones.at[own_place],
            send_sem=cell_send,
            recv_sem=cell_recv,
            device_id={"cell": alike(step)},
            device_id_type=MESH,
        ).start()
    pltpu.make_async_copy(mine, everyones.at[own_place], cell_recv).start()
    arrived(everyones, cell_recv)
    everything = jnp.sum(everyones[...], axis=(0, 1))
    for h in range(heads):
        square[h : h + 1, :] = everything[h]
    slot_rows = lax.broadcasted_iota(jnp.int32, (BLOCK, BLOCK), 0)
    picked = jnp.sum(jnp.where(slot_rows == cell, square[...].T, 0.0), axis=0, keepdims=True)
    bias_out[0] = picked[:, 0:heads]

    for a, out in enumerate((dq_out, dk_out, dv_out)):
        arrived(out, out_recv.at[a])

    def sent(ref, count, sem):
        part = ref.at[pl.ds(0, count)]
        pltpu.make_async_copy(part, part, sem).wait()

    for a in range(4):
        sent(kf, heads * BLOCK, in_send.at[a])
    sent(statf, heads, in_send.at[4])

    @pl.when(active)
    def _():
        for a in range(3):
            sent(dq, genes * BLOCK, out_send.at[a])
        sent(terms, genes, term_send.at[0])
        sent(terms, genes - 1, term_send.at[1])

    @pl.when(jnp.logical_not(active))
    def _():
        sent(dv, genes * BLOCK, out_send.at[2])
        sent(dq, RELAYED * BLOCK, out_send.at[0])

    sent(everyones, cells // 2 - 1, cell_send)


def put_out(*refs):
    count = (len(refs) - 1) // 2
    copies = [
        pltpu.make_async_copy(refs[n], refs[count + n], refs[-1].at[n]) for n in range(count)
    ]
    for copy in copies:
        copy.start()
    for copy in copies:
        copy.wait()


def shards(
    query_rows,
    key_rows,
    value_rows,
    output_rows,
    output_grad,
    row_lse,
    block_bias,
    block_index,
    block_count,
):
    heads = row_lse.shape[2]
    genes = block_index.shape[0]
    cells = lax.axis_size("cell")
    rows = genes * BLOCK
    anywhere = pl.BlockSpec(memory_space=pl.ANY)
    vmem = pl.BlockSpec(memory_space=pltpu.VMEM)
    flat = jax.ShapeDtypeStruct(query_rows.shape, BF16)
    dma = pltpu.SemaphoreType.DMA
    wides = rows // WIDE
    held = pltpu.VMEM(query_rows.shape, BF16)
    bias_flat = (1, 1, heads)
    results = pl.pallas_call(
        functools.partial(kernel, heads, genes, cells),
        out_shape=(held, held, held, pltpu.VMEM(bias_flat, F32)),
        in_specs=[pl.BlockSpec(memory_space=pltpu.HBM)] * 9,
        out_specs=(vmem, vmem, vmem, vmem),
        scratch_shapes=[
            pltpu.VMEM((rows, BLOCK), BF16),
            pltpu.VMEM((rows, BLOCK), BF16),
            pltpu.VMEM((rows, BLOCK), BF16),
            pltpu.VMEM((rows, BLOCK), BF16),
            pltpu.VMEM((genes, 2, BLOCK), F32),
            pltpu.VMEM((BLOCK, heads * BLOCK), BF16),
            pltpu.VMEM((BLOCK, heads * BLOCK), BF16),
            pltpu.VMEM((heads, 2, BLOCK), F32),
            pltpu.VMEM((BLOCK, BLOCK), F32),
            pltpu.VMEM((BLOCK, rows), BF16),
            pltpu.VMEM((wides, genes, WIDE), F32),
            pltpu.VMEM((wides, rows, WIDE), F32),
            pltpu.VMEM((wides, rows, WIDE), BF16),
            pltpu.VMEM((wides, genes, WIDE), F32),
            pltpu.VMEM((rows, BLOCK), BF16),
            pltpu.VMEM((rows, BLOCK), BF16),
            pltpu.VMEM((rows, BLOCK), BF16),
            pltpu.VMEM((genes, 1, BLOCK), F32),
            pltpu.VMEM((2, heads, 1, BLOCK), F32),
            pltpu.VMEM((cells // 2, 2, heads, 1, BLOCK), F32),
            pltpu.VMEM((3, RELAYED * BLOCK, BLOCK), BF16),
            pltpu.VMEM((heads, 1, BLOCK), F32),
            pltpu.VMEM((heads, genes, genes), F32),
            pltpu.VMEM((genes, genes), jnp.int32),
            pltpu.SMEM((genes,), jnp.int32),
            dma((6,)),
            dma((5,)),
            dma((5,)),
            dma((SIDE,)),
            dma((3,)),
            dma((3,)),
            dma((3,)),
            dma((2,)),
            dma,
            dma,
            dma,
        ],
        compiler_params=pltpu.CompilerParams(
            collective_id=0, has_side_effects=True, vmem_limit_bytes=60 * 1024 * 1024
        ),
    )(
        query_rows,
        key_rows,
        value_rows,
        output_rows,
        output_grad,
        jnp.transpose(row_lse, (2, 0, 1)),
        jnp.transpose(block_bias, (1, 0, 2)),
        block_index,
        block_count,
    )
    query_grad, key_grad, value_grad, bias_grad = pl.pallas_call(
        put_out,
        out_shape=(flat, flat, flat, jax.ShapeDtypeStruct(bias_flat, F32)),
        in_specs=[anywhere] * 4,
        out_specs=(anywhere,) * 4,
        scratch_shapes=[dma((4,))],
        compiler_params=pltpu.CompilerParams(vmem_limit_bytes=1024 * 1024),
    )(*(pltpu.with_memory_space_constraint(r, pltpu.VMEM) for r in results))
    return (query_grad, key_grad, value_grad, jnp.transpose(bias_grad, (0, 2, 1)))


def solution(mesh):
    in_specs = (
        P("cell", "gene", None),
        P("cell", "gene", None),
        P("cell", "gene", None),
        P("cell", "gene", None),
        P("cell", "gene", None),
        P("cell", "gene", None),
        P(),
        P(),
        P(),
    )
    out_specs = (
        P("cell", "gene", None),
        P("cell", "gene", None),
        P("cell", "gene", None),
        P("gene", None, "cell"),
    )
    return jax.shard_map(shards, mesh=mesh, in_specs=in_specs, out_specs=out_specs, check_vma=False)
```

```python
import functools
import math

import jax
import jax.numpy as jnp
from jax import lax
from jax.experimental import pallas as pl
from jax.experimental.pallas import tpu as pltpu
from jax.sharding import PartitionSpec as P

MESH = pl.DeviceIdType.MESH
BLOCK = 128
SIDE = 4
WIDE = 256
TALL = 512
UNROLL = 4
RELAYED = 4
LOG2E = 1.4426950408889634
OFF = -1.0e30
BF16 = jnp.bfloat16
F32 = jnp.float32


def nt_dot(a, b):
    return lax.dot_general(a, b, (((1,), (1,)), ((), ())), preferred_element_type=F32)


def nn_dot(a, b):
    return jnp.dot(a, b, preferred_element_type=F32)


def kernel(
    heads,
    genes,
    cells,
    q_in,
    k_in,
    v_in,
    o_in,
    g_in,
    lse_in,
    bias_in,
    index_in,
    count_in,
    dq_out,
    dk_out,
    dv_out,
    bias_out,
    qf,
    kf,
    vf,
    gf,
    statf,
    o_own,
    g_own,
    stat,
    square,
    kt,
    addend,
    weights,
    low,
    colsum,
    dq,
    dk,
    dv,
    terms,
    mine,
    everyones,
    relay,
    lse_own,
    bias_own,
    index_own,
    count_own,
    load_sem,
    in_send,
    in_recv,
    v_recv,
    out_send,
    out_recv,
    relay_recv,
    term_send,
    term_recv,
    cell_send,
    cell_recv,
):
    gene = lax.axis_index("gene")
    cell = lax.axis_index("cell")
    row, col = gene // SIDE, gene % SIDE
    core, half = cell % 2, (cell // 2) % 2
    way = 2 * half - 1
    other = cell + 2 - 4 * half
    live_heads = heads // SIDE
    scale = 1.0 / math.sqrt(BLOCK)

    def slot_of(r, side):
        return (r + 2 * core + side) % SIDE

    def device_at(to):
        return {"cell": other, "gene": to}

    place = slot_of(row, half)
    active = place < live_heads
    head = live_heads * col + place
    head_cols = pl.ds(pl.multiple_of(head * BLOCK, BLOCK), BLOCK)

    beside_row = row + 1 - 2 * (row % 2)
    beside = beside_row * SIDE + col
    beside_place = slot_of(beside_row, half)
    helped = jnp.logical_and(active, beside_place >= live_heads)
    beside_cols = pl.ds(
        pl.multiple_of((live_heads * col + beside_place) * BLOCK, BLOCK), BLOCK
    )

    def peer(step):
        r, c = (row + step // SIDE) % SIDE, (col + step % SIDE) % SIDE
        return r, c, r * SIDE + c

    def block_of(i):
        return pl.ds(pl.multiple_of(i * BLOCK, BLOCK), BLOCK)

    barrier = pltpu.get_barrier_semaphore()
    def alike(step):
        return (cell // 4 + step // 2) % (cells // 4) * 4 + 2 * half + (core + step) % 2

    def hops(entry):
        theirs, down, over = entry
        along = (1, 1, 3, 3)[over] if theirs else (0, 2, 4, 2)[over]
        return min(down, SIDE - down) + along

    greeted = [(t, d, e) for t in (True, False) for d in range(SIDE) for e in range(SIDE)]
    for theirs, down, over in sorted(greeted, key=hops, reverse=True):
        r, c = (row + down) % SIDE, (col + over * way + SIDE) % SIDE
        to = r * SIDE + c
        if theirs:
            pl.semaphore_signal(barrier, inc=1, device_id=device_at(to), device_id_type=MESH)
        elif down + over > 0:
            pl.semaphore_signal(barrier, inc=1, device_id={"gene": to}, device_id_type=MESH)
    for step in range(1, cells // 2):
        pl.semaphore_signal(barrier, inc=1, device_id={"cell": alike(step)}, device_id_type=MESH)

    loads = [
        pltpu.make_async_copy(src, dst, load_sem.at[n])
        for n, (src, dst) in enumerate(
            (
                (o_in.at[0], o_own),
                (g_in.at[0], g_own),
                (lse_in, lse_own),
                (bias_in, bias_own),
                (index_in, index_own),
                (count_in, count_own),
            )
        )
    ]
    for load in loads:
        load.start()
    pl.semaphore_wait(barrier, 2 * genes + cells // 2 - 2)

    moved = ((k_in, kf), (q_in, qf), (g_in, gf), (v_in, vf))

    def send_array(a, src, dst, recv_sem):
        for step in range(genes):
            r, c, to = peer(step)
            spot = slot_of(r, 1 - half)

            @pl.when(spot < live_heads)
            def _():
                cols = pl.ds(pl.multiple_of((live_heads * c + spot) * BLOCK, BLOCK), BLOCK)
                pltpu.make_async_remote_copy(
                    src_ref=src.at[0, :, cols],
                    dst_ref=dst.at[block_of(gene), :],
                    send_sem=in_send.at[a],
                    recv_sem=recv_sem,
                    device_id=device_at(to),
                    device_id_type=MESH,
                ).start()

    send_array(0, *moved[0], in_recv.at[0])
    send_array(1, *moved[1], in_recv.at[1])
    terms[...] = jnp.zeros_like(terms)
    lanes = lax.broadcasted_iota(jnp.int32, (BLOCK, BLOCK), 1)
    for load in loads:
        load.wait()
    deltas = jnp.zeros((BLOCK, BLOCK), F32)
    for h in range(heads):
        cols = slice(h * BLOCK, (h + 1) * BLOCK)
        one = jnp.sum(
            g_own[:, cols].astype(F32) * o_own[:, cols].astype(F32), axis=1, keepdims=True
        )
        deltas = jnp.where(lanes == h, one, deltas)
    turned = deltas.T
    for h in range(heads):
        stat[h, 0:1, :] = lse_own[h]
        stat[h, 1:2, :] = turned[h : h + 1, :]

    for step in range(genes):
        r, c, to = peer(step)
        spot = slot_of(r, 1 - half)

        @pl.when(spot < live_heads)
        def _():
            pltpu.make_async_remote_copy(
                src_ref=stat.at[live_heads * c + spot],
                dst_ref=statf.at[gene],
                send_sem=in_send.at[4],
                recv_sem=in_recv.at[4],
                device_id=device_at(to),
                device_id_type=MESH,
            ).start()

    send_array(2, *moved[2], in_recv.at[2])
    send_array(3, *moved[3], v_recv.at[row])

    def arrived(ref, sem):
        pltpu.make_async_copy(ref, ref, sem).wait()

    def give_direct(a, src, dst, to):
        pltpu.make_async_remote_copy(
            src_ref=src.at[block_of(to), :],
            dst_ref=dst.at[0, :, head_cols],
            send_sem=out_send.at[a],
            recv_sem=out_recv.at[a],
            device_id=device_at(to),
            device_id_type=MESH,
        ).start()

    wides = genes * BLOCK // WIDE
    per_wide = WIDE // BLOCK

    def wide_at(step):
        return (gene // per_wide + step) % wides

    def wide_of(n):
        return pl.ds(pl.multiple_of(n * WIDE, WIDE), WIDE)

    lap = RELAYED // per_wide

    def early_at(step):
        return lax.shift_right_logical(jnp.int32(16096528), jnp.int32(3) * step) % wides

    def give_keys(step):
        for b in range(per_wide):
            give_direct(1, dk, dk_out, early_at(step) * per_wide + b)

    def give_wide_back(a, src, dst, step, relayed, stage):
        for b in range(per_wide):
            to = wide_at(step) * per_wide + b
            by_relay = jnp.logical_and(helped, step < relayed)

            @pl.when(by_relay)
            def _():
                pltpu.make_async_remote_copy(
                    src_ref=src.at[block_of(to), :],
                    dst_ref=relay.at[stage + step // lap, block_of(step % lap * per_wide + b), :],
                    send_sem=out_send.at[a],
                    recv_sem=relay_recv.at[stage + step // lap],
                    device_id={"gene": beside},
                    device_id_type=MESH,
                ).start()

            @pl.when(jnp.logical_not(by_relay))
            def _():
                give_direct(a, src, dst, to)

    def pass_on(a, dst, stage, first):
        arrived(relay.at[stage], relay_recv.at[stage])
        for k in range(RELAYED):
            m = (beside // per_wide + first + k // per_wide) % wides
            pltpu.make_async_remote_copy(
                src_ref=relay.at[stage, block_of(k), :],
                dst_ref=dst.at[0, :, beside_cols],
                send_sem=out_send.at[a],
                recv_sem=out_recv.at[a],
                device_id=device_at(m * per_wide + k % per_wide),
                device_id_type=MESH,
            ).start()

    def over_queries(m, right):
        total = jnp.zeros((WIDE, BLOCK), F32)
        for n in range(wides):
            total = total + nn_dot(low[n, wide_of(m), :], right[n * WIDE : (n + 1) * WIDE, :])
        return total

    keys_iota = lax.broadcasted_iota(jnp.int32, (genes, genes), 0)
    slot_iota = lax.broadcasted_iota(jnp.int32, (genes, genes), 1)

    def listed(i):
        return (index_own[i : i + 1, :] == keys_iota) & (slot_iota < count_own[i])

    @pl.when(active)
    def _():
        arrived(statf, in_recv.at[4])
        for i in range(genes):
            hit = listed(i)
            bias_row = bias_own[head, i : i + 1, :]
            bias_col = jnp.sum(jnp.where(hit, bias_row, 0.0), axis=1, keepdims=True)
            hit_col = jnp.sum(jnp.where(hit, 1.0, 0.0), axis=1, keepdims=True)
            start = jnp.where(hit_col > 0.5, bias_col * LOG2E, OFF)
            n, at = i // per_wide, i % per_wide * BLOCK
            addend[n, :, at : at + BLOCK] = start - statf[i, 0:1, :] * LOG2E
        arrived(kf, in_recv.at[0])

        def turn_keys(i, carry):
            kt[:, block_of(i)] = kf[block_of(i), :].T
            return carry

        lax.fori_loop(0, genes, turn_keys, 0)
        arrived(qf, in_recv.at[1])

        def score_step(n, carry):
            own = qf[wide_of(n), :]
            for m in range(0, genes * BLOCK, TALL):
                scores = nt_dot(kf[m : m + TALL, :], own)
                for b in range(0, TALL, BLOCK):
                    j = (m + b) // BLOCK
                    span = slice(m + b, m + b + BLOCK)
                    w = jnp.exp2(
                        scores[b : b + BLOCK, :] * (scale * LOG2E) + addend[n, j : j + 1, :]
                    )
                    weights[n, span, :] = w
                    low[n, span, :] = w.astype(BF16)
            return carry

        lax.fori_loop(0, wides, score_step, 0)
        arrived(gf, in_recv.at[2])

        def value_step(step, carry):
            m = wide_at(step)
            dv[wide_of(m), :] = over_queries(m, gf).astype(BF16)

            @pl.when(step > 0)
            def _():
                give_wide_back(2, dv, dv_out, step - 1, wides, 0)

            return carry

        lax.fori_loop(0, wides, value_step, 0)
        give_wide_back(2, dv, dv_out, wides - 1, wides, 0)

        def part_step(k, carry):
            part = (row + SIDE - k) % SIDE
            keys = pl.ds(pl.multiple_of(part * TALL, TALL), TALL)
            arrived(vf.at[keys, :], v_recv.at[part])

            def grad_step(lap, inner):
                for n in [lap * UNROLL + u for u in range(UNROLL)]:
                    delta = jnp.concatenate(
                        [statf[n * per_wide + b, 1:2, :] for b in range(per_wide)], axis=1
                    )
                    wg = nt_dot(vf[keys, :], gf[wide_of(n), :])
                    for b in range(TALL // BLOCK):
                        j = part * (TALL // BLOCK) + b
                        ds = weights[n, block_of(j), :] * (
                            wg[b * BLOCK : (b + 1) * BLOCK, :] - delta
                        )
                        colsum[n, pl.ds(j, 1), :] = jnp.sum(ds, axis=0, keepdims=True)
                        low[n, block_of(j), :] = ds.astype(BF16)
                return inner

            return lax.fori_loop(0, wides // UNROLL, grad_step, carry)

        lax.fori_loop(0, SIDE, part_step, 0)
        for i in range(genes):
            n, at = i // per_wide, i % per_wide * BLOCK
            sums = jnp.sum(colsum[n, :, at : at + BLOCK], axis=1, keepdims=True)
            terms[i, :, 0:genes] = jnp.sum(jnp.where(listed(i), sums, 0.0), axis=0, keepdims=True)

        def query_step(step, carry):
            n = wide_at(step)
            across = nn_dot(kt[...], low[n])
            dq[wide_of(n), :] = (across.T * scale).astype(BF16)

            @pl.when(step > 0)
            def _():
                give_wide_back(0, dq, dq_out, step - 1, wides // 2, 4)

            @pl.when(step == 0)
            def _():
                for to_step in range(genes):
                    to = peer(to_step)[2]
                    pltpu.make_async_remote_copy(
                        src_ref=terms.at[to],
                        dst_ref=mine.at[1 - half, head],
                        send_sem=term_send.at[0],
                        recv_sem=term_recv,
                        device_id=device_at(to),
                        device_id_type=MESH,
                    ).start()
                    if to_step > 0:
                        pltpu.make_async_remote_copy(
                            src_ref=terms.at[to],
                            dst_ref=mine.at[1 - half, head],
                            send_sem=term_send.at[1],
                            recv_sem=term_recv,
                            device_id={"gene": to},
                            device_id_type=MESH,
                        ).start()
                pltpu.make_async_copy(terms.at[gene], mine.at[1 - half, head], term_recv).start()

            return carry

        lax.fori_loop(0, wides, query_step, 0)
        give_wide_back(0, dq, dq_out, wides - 1, wides // 2, 4)

        def key_step(step, carry):
            m = early_at(step)
            dk[wide_of(m), :] = (over_queries(m, qf) * scale).astype(BF16)

            @pl.when(step > 0)
            def _():
                give_keys(step - 1)

            return carry

        lax.fori_loop(0, wides, key_step, 0)
        give_keys(wides - 1)
    @pl.when(jnp.logical_not(active))
    def _():
        for part in range(4):
            pass_on(2, dv_out, part, part * lap)
        for part in range(2):
            pass_on(0, dq_out, 4 + part, part * lap)

    square[...] = jnp.zeros_like(square)
    arrived(mine, term_recv)
    own_place = cell // 4 * 2 + core
    for step in range(1, cells // 2):
        pltpu.make_async_remote_copy(
            src_ref=mine,
            dst_ref=everyones.at[own_place],
            send_sem=cell_send,
            recv_sem=cell_recv,
            device_id={"cell": alike(step)},
            device_id_type=MESH,
        ).start()
    pltpu.make_async_copy(mine, everyones.at[own_place], cell_recv).start()
    arrived(everyones, cell_recv)
    everything = jnp.sum(everyones[...], axis=(0, 1))
    for h in range(heads):
        square[h : h + 1, :] = everything[h]
    slot_rows = lax.broadcasted_iota(jnp.int32, (BLOCK, BLOCK), 0)
    picked = jnp.sum(jnp.where(slot_rows == cell, square[...].T, 0.0), axis=0, keepdims=True)
    bias_out[0] = picked[:, 0:heads]

    for a, out in enumerate((dq_out, dk_out, dv_out)):
        arrived(out, out_recv.at[a])

    def sent(ref, count, sem):
        part = ref.at[pl.ds(0, count)]
        pltpu.make_async_copy(part, part, sem).wait()

    for a in range(4):
        sent(kf, heads * BLOCK, in_send.at[a])
    sent(statf, heads, in_send.at[4])

    @pl.when(active)
    def _():
        for a in range(3):
            sent(dq, genes * BLOCK, out_send.at[a])
        sent(terms, genes, term_send.at[0])
        sent(terms, genes - 1, term_send.at[1])

    @pl.when(jnp.logical_not(active))
    def _():
        sent(dv, genes * BLOCK, out_send.at[2])
        sent(dq, genes // 2 * BLOCK, out_send.at[0])

    sent(everyones, cells // 2 - 1, cell_send)


def put_out(*refs):
    count = (len(refs) - 1) // 2
    copies = [
        pltpu.make_async_copy(refs[n], refs[count + n], refs[-1].at[n]) for n in range(count)
    ]
    for copy in copies:
        copy.start()
    for copy in copies:
        copy.wait()


def shards(
    query_rows,
    key_rows,
    value_rows,
    output_rows,
    output_grad,
    row_lse,
    block_bias,
    block_index,
    block_count,
):
    heads = row_lse.shape[2]
    genes = block_index.shape[0]
    cells = lax.axis_size("cell")
    rows = genes * BLOCK
    anywhere = pl.BlockSpec(memory_space=pl.ANY)
    vmem = pl.BlockSpec(memory_space=pltpu.VMEM)
    flat = jax.ShapeDtypeStruct(query_rows.shape, BF16)
    dma = pltpu.SemaphoreType.DMA
    wides = rows // WIDE
    held = pltpu.VMEM(query_rows.shape, BF16)
    bias_flat = (1, 1, heads)
    results = pl.pallas_call(
        functools.partial(kernel, heads, genes, cells),
        out_shape=(held, held, held, pltpu.VMEM(bias_flat, F32)),
        in_specs=[pl.BlockSpec(memory_space=pltpu.HBM)] * 9,
        out_specs=(vmem, vmem, vmem, vmem),
        scratch_shapes=[
            pltpu.VMEM((rows, BLOCK), BF16),
            pltpu.VMEM((rows, BLOCK), BF16),
            pltpu.VMEM((rows, BLOCK), BF16),
            pltpu.VMEM((rows, BLOCK), BF16),
            pltpu.VMEM((genes, 2, BLOCK), F32),
            pltpu.VMEM((BLOCK, heads * BLOCK), BF16),
            pltpu.VMEM((BLOCK, heads * BLOCK), BF16),
            pltpu.VMEM((heads, 2, BLOCK), F32),
            pltpu.VMEM((BLOCK, BLOCK), F32),
            pltpu.VMEM((BLOCK, rows), BF16),
            pltpu.VMEM((wides, genes, WIDE), F32),
            pltpu.VMEM((wides, rows, WIDE), F32),
            pltpu.VMEM((wides, rows, WIDE), BF16),
            pltpu.VMEM((wides, genes, WIDE), F32),
            pltpu.VMEM((rows, BLOCK), BF16),
            pltpu.VMEM((rows, BLOCK), BF16),
            pltpu.VMEM((rows, BLOCK), BF16),
            pltpu.VMEM((genes, 1, BLOCK), F32),
            pltpu.VMEM((2, heads, 1, BLOCK), F32),
            pltpu.VMEM((cells // 2, 2, heads, 1, BLOCK), F32),
            pltpu.VMEM((6, RELAYED * BLOCK, BLOCK), BF16),
            pltpu.VMEM((heads, 1, BLOCK), F32),
            pltpu.VMEM((heads, genes, genes), F32),
            pltpu.VMEM((genes, genes), jnp.int32),
            pltpu.SMEM((genes,), jnp.int32),
            dma((6,)),
            dma((5,)),
            dma((5,)),
            dma((SIDE,)),
            dma((3,)),
            dma((3,)),
            dma((6,)),
            dma((2,)),
            dma,
            dma,
            dma,
        ],
        compiler_params=pltpu.CompilerParams(
            collective_id=0, has_side_effects=True, vmem_limit_bytes=60 * 1024 * 1024
        ),
    )(
        query_rows,
        key_rows,
        value_rows,
        output_rows,
        output_grad,
        jnp.transpose(row_lse, (2, 0, 1)),
        jnp.transpose(block_bias, (1, 0, 2)),
        block_index,
        block_count,
    )
    query_grad, key_grad, value_grad, bias_grad = pl.pallas_call(
        put_out,
        out_shape=(flat, flat, flat, jax.ShapeDtypeStruct(bias_flat, F32)),
        in_specs=[anywhere] * 4,
        out_specs=(anywhere,) * 4,
        scratch_shapes=[dma((4,))],
        compiler_params=pltpu.CompilerParams(vmem_limit_bytes=1024 * 1024),
    )(*(pltpu.with_memory_space_constraint(r, pltpu.VMEM) for r in results))
    return (query_grad, key_grad, value_grad, jnp.transpose(bias_grad, (0, 2, 1)))


def solution(mesh):
    in_specs = (
        P("cell", "gene", None),
        P("cell", "gene", None),
        P("cell", "gene", None),
        P("cell", "gene", None),
        P("cell", "gene", None),
        P("cell", "gene", None),
        P(),
        P(),
        P(),
    )
    out_specs = (
        P("cell", "gene", None),
        P("cell", "gene", None),
        P("cell", "gene", None),
        P("gene", None, "cell"),
    )
    return jax.shard_map(shards, mesh=mesh, in_specs=in_specs, out_specs=out_specs, check_vma=False)
```

```python
import functools
import math

import jax
import jax.numpy as jnp
from jax import lax
from jax.experimental import pallas as pl
from jax.experimental.pallas import tpu as pltpu
from jax.sharding import PartitionSpec as P

MESH = pl.DeviceIdType.MESH
BLOCK = 128
SIDE = 4
WIDE = 256
TALL = 512
UNROLL = 4
RELAYED = 4
LOG2E = 1.4426950408889634
OFF = -1.0e30
BF16 = jnp.bfloat16
F32 = jnp.float32


def nt_dot(a, b):
    return lax.dot_general(a, b, (((1,), (1,)), ((), ())), preferred_element_type=F32)


def nn_dot(a, b):
    return jnp.dot(a, b, preferred_element_type=F32)


def kernel(
    heads,
    genes,
    cells,
    q_in,
    k_in,
    v_in,
    o_in,
    g_in,
    lse_in,
    bias_in,
    index_in,
    count_in,
    dq_out,
    dk_out,
    dv_out,
    bias_out,
    qf,
    kf,
    vf,
    gf,
    statf,
    o_own,
    g_own,
    stat,
    square,
    kt,
    addend,
    weights,
    low,
    colsum,
    dq,
    dk,
    dv,
    terms,
    mine,
    everyones,
    relay,
    lse_own,
    bias_own,
    index_own,
    count_own,
    load_sem,
    in_send,
    in_recv,
    v_recv,
    out_send,
    out_recv,
    relay_recv,
    term_send,
    term_recv,
    cell_send,
    cell_recv,
):
    gene = lax.axis_index("gene")
    cell = lax.axis_index("cell")
    row, col = gene // SIDE, gene % SIDE
    core, half = cell % 2, (cell // 2) % 2
    way = 2 * half - 1
    other = cell + 2 - 4 * half
    live_heads = heads // SIDE
    scale = 1.0 / math.sqrt(BLOCK)

    def slot_of(r, side):
        return (r + 2 * core + side) % SIDE

    def device_at(to):
        return {"cell": other, "gene": to}

    place = slot_of(row, half)
    active = place < live_heads
    head = live_heads * col + place
    head_cols = pl.ds(pl.multiple_of(head * BLOCK, BLOCK), BLOCK)

    beside_row = row + 1 - 2 * (row % 2)
    beside = beside_row * SIDE + col
    beside_place = slot_of(beside_row, half)
    helped = jnp.logical_and(active, beside_place >= live_heads)
    beside_cols = pl.ds(
        pl.multiple_of((live_heads * col + beside_place) * BLOCK, BLOCK), BLOCK
    )

    def peer(step):
        r, c = (row + step // SIDE) % SIDE, (col + step % SIDE) % SIDE
        return r, c, r * SIDE + c

    def block_of(i):
        return pl.ds(pl.multiple_of(i * BLOCK, BLOCK), BLOCK)

    barrier = pltpu.get_barrier_semaphore()
    def alike(step):
        return (cell // 4 + step // 2) % (cells // 4) * 4 + 2 * half + (core + step) % 2

    def hops(entry):
        theirs, down, over = entry
        along = (1, 1, 3, 3)[over] if theirs else (0, 2, 4, 2)[over]
        return min(down, SIDE - down) + along

    greeted = [(t, d, e) for t in (True, False) for d in range(SIDE) for e in range(SIDE)]
    for theirs, down, over in sorted(greeted, key=hops, reverse=True):
        r, c = (row + down) % SIDE, (col + over * way + SIDE) % SIDE
        to = r * SIDE + c
        if theirs:
            pl.semaphore_signal(barrier, inc=1, device_id=device_at(to), device_id_type=MESH)
        elif down + over > 0:
            pl.semaphore_signal(barrier, inc=1, device_id={"gene": to}, device_id_type=MESH)
    for step in range(1, cells // 2):
        pl.semaphore_signal(barrier, inc=1, device_id={"cell": alike(step)}, device_id_type=MESH)

    loads = [
        pltpu.make_async_copy(src, dst, load_sem.at[n])
        for n, (src, dst) in enumerate(
            (
                (o_in.at[0], o_own),
                (g_in.at[0], g_own),
                (lse_in, lse_own),
                (bias_in, bias_own),
                (index_in, index_own),
                (count_in, count_own),
            )
        )
    ]
    for load in loads:
        load.start()
    pl.semaphore_wait(barrier, 2 * genes + cells // 2 - 2)

    moved = ((k_in, kf), (q_in, qf), (g_in, gf), (v_in, vf))

    def send_array(a, src, dst, recv_sem):
        for k in range(genes):
            down, e = k // 2 % SIDE, k // (2 * SIDE) * 2 + k % 2
            if src is v_in:
                down, e = k // SIDE, k % SIDE
            r, c = (row + down) % SIDE, (col + e * way + SIDE) % SIDE
            to = r * SIDE + c
            spot = slot_of(r, 1 - half)

            @pl.when(spot < live_heads)
            def _():
                cols = pl.ds(pl.multiple_of((live_heads * c + spot) * BLOCK, BLOCK), BLOCK)
                pltpu.make_async_remote_copy(
                    src_ref=src.at[0, :, cols],
                    dst_ref=dst.at[block_of(gene), :],
                    send_sem=in_send.at[a],
                    recv_sem=recv_sem,
                    device_id=device_at(to),
                    device_id_type=MESH,
                ).start()

    send_array(0, *moved[0], in_recv.at[0])
    send_array(1, *moved[1], in_recv.at[1])
    terms[...] = jnp.zeros_like(terms)
    lanes = lax.broadcasted_iota(jnp.int32, (BLOCK, BLOCK), 1)
    for load in loads:
        load.wait()
    deltas = jnp.zeros((BLOCK, BLOCK), F32)
    for h in range(heads):
        cols = slice(h * BLOCK, (h + 1) * BLOCK)
        one = jnp.sum(
            g_own[:, cols].astype(F32) * o_own[:, cols].astype(F32), axis=1, keepdims=True
        )
        deltas = jnp.where(lanes == h, one, deltas)
    turned = deltas.T
    for h in range(heads):
        stat[h, 0:1, :] = lse_own[h]
        stat[h, 1:2, :] = turned[h : h + 1, :]

    for step in range(genes):
        r, c, to = peer(step)
        spot = slot_of(r, 1 - half)

        @pl.when(spot < live_heads)
        def _():
            pltpu.make_async_remote_copy(
                src_ref=stat.at[live_heads * c + spot],
                dst_ref=statf.at[gene],
                send_sem=in_send.at[4],
                recv_sem=in_recv.at[4],
                device_id=device_at(to),
                device_id_type=MESH,
            ).start()

    send_array(2, *moved[2], in_recv.at[2])
    send_array(3, *moved[3], v_recv.at[row])

    def arrived(ref, sem):
        pltpu.make_async_copy(ref, ref, sem).wait()

    def give_direct(a, src, dst, to):
        pltpu.make_async_remote_copy(
            src_ref=src.at[block_of(to), :],
            dst_ref=dst.at[0, :, head_cols],
            send_sem=out_send.at[a],
            recv_sem=out_recv.at[a],
            device_id=device_at(to),
            device_id_type=MESH,
        ).start()

    wides = genes * BLOCK // WIDE
    per_wide = WIDE // BLOCK

    def wide_at(step):
        return (gene // per_wide + step) % wides

    def wide_of(n):
        return pl.ds(pl.multiple_of(n * WIDE, WIDE), WIDE)

    lap = RELAYED // per_wide

    def early_at(step):
        return lax.shift_right_logical(jnp.int32(16096528), jnp.int32(3) * step) % wides

    def give_keys(step):
        for b in range(per_wide):
            give_direct(1, dk, dk_out, early_at(step) * per_wide + b)

    def give_wide_back(a, src, dst, step, relayed, stage):
        for b in range(per_wide):
            to = wide_at(step) * per_wide + b
            by_relay = jnp.logical_and(helped, step < relayed)

            @pl.when(by_relay)
            def _():
                pltpu.make_async_remote_copy(
                    src_ref=src.at[block_of(to), :],
                    dst_ref=relay.at[stage + step // lap, block_of(step % lap * per_wide + b), :],
                    send_sem=out_send.at[a],
                    recv_sem=relay_recv.at[stage + step // lap],
                    device_id={"gene": beside},
                    device_id_type=MESH,
                ).start()

            @pl.when(jnp.logical_not(by_relay))
            def _():
                give_direct(a, src, dst, to)

    def pass_on(a, dst, stage, first):
        arrived(relay.at[stage], relay_recv.at[stage])
        for k in range(RELAYED):
            m = (beside // per_wide + first + k // per_wide) % wides
            pltpu.make_async_remote_copy(
                src_ref=relay.at[stage, block_of(k), :],
                dst_ref=dst.at[0, :, beside_cols],
                send_sem=out_send.at[a],
                recv_sem=out_recv.at[a],
                device_id=device_at(m * per_wide + k % per_wide),
                device_id_type=MESH,
            ).start()

    def over_queries(m, right):
        total = jnp.zeros((WIDE, BLOCK), F32)
        for n in range(wides):
            total = total + nn_dot(low[n, wide_of(m), :], right[n * WIDE : (n + 1) * WIDE, :])
        return total

    keys_iota = lax.broadcasted_iota(jnp.int32, (genes, genes), 0)
    slot_iota = lax.broadcasted_iota(jnp.int32, (genes, genes), 1)

    def listed(i):
        return (index_own[i : i + 1, :] == keys_iota) & (slot_iota < count_own[i])

    @pl.when(active)
    def _():
        arrived(statf, in_recv.at[4])
        for i in range(genes):
            hit = listed(i)
            bias_row = bias_own[head, i : i + 1, :]
            bias_col = jnp.sum(jnp.where(hit, bias_row, 0.0), axis=1, keepdims=True)
            hit_col = jnp.sum(jnp.where(hit, 1.0, 0.0), axis=1, keepdims=True)
            start = jnp.where(hit_col > 0.5, bias_col * LOG2E, OFF)
            n, at = i // per_wide, i % per_wide * BLOCK
            addend[n, :, at : at + BLOCK] = start - statf[i, 0:1, :] * LOG2E
        arrived(kf, in_recv.at[0])

        def turn_keys(i, carry):
            kt[:, block_of(i)] = kf[block_of(i), :].T
            return carry

        lax.fori_loop(0, genes, turn_keys, 0)
        arrived(qf, in_recv.at[1])

        def score_step(n, carry):
            own = qf[wide_of(n), :]
            for m in range(0, genes * BLOCK, TALL):
                scores = nt_dot(kf[m : m + TALL, :], own)
                for b in range(0, TALL, BLOCK):
                    j = (m + b) // BLOCK
                    span = slice(m + b, m + b + BLOCK)
                    w = jnp.exp2(
                        scores[b : b + BLOCK, :] * (scale * LOG2E) + addend[n, j : j + 1, :]
                    )
                    weights[n, span, :] = w
                    low[n, span, :] = w.astype(BF16)
            return carry

        lax.fori_loop(0, wides, score_step, 0)
        arrived(gf, in_recv.at[2])

        def value_step(step, carry):
            m = wide_at(step)
            dv[wide_of(m), :] = over_queries(m, gf).astype(BF16)

            @pl.when(step > 0)
            def _():
                give_wide_back(2, dv, dv_out, step - 1, wides, 0)

            return carry

        lax.fori_loop(0, wides, value_step, 0)
        give_wide_back(2, dv, dv_out, wides - 1, wides, 0)

        def part_step(k, carry):
            part = (row + SIDE - k) % SIDE
            keys = pl.ds(pl.multiple_of(part * TALL, TALL), TALL)
            arrived(vf.at[keys, :], v_recv.at[part])

            def grad_step(lap, inner):
                for n in [lap * UNROLL + u for u in range(UNROLL)]:
                    delta = jnp.concatenate(
                        [statf[n * per_wide + b, 1:2, :] for b in range(per_wide)], axis=1
                    )
                    wg = nt_dot(vf[keys, :], gf[wide_of(n), :])
                    for b in range(TALL // BLOCK):
                        j = part * (TALL // BLOCK) + b
                        ds = weights[n, block_of(j), :] * (
                            wg[b * BLOCK : (b + 1) * BLOCK, :] - delta
                        )
                        colsum[n, pl.ds(j, 1), :] = jnp.sum(ds, axis=0, keepdims=True)
                        low[n, block_of(j), :] = ds.astype(BF16)
                return inner

            return lax.fori_loop(0, wides // UNROLL, grad_step, carry)

        lax.fori_loop(0, SIDE, part_step, 0)
        for i in range(genes):
            n, at = i // per_wide, i % per_wide * BLOCK
            sums = jnp.sum(colsum[n, :, at : at + BLOCK], axis=1, keepdims=True)
            terms[i, :, 0:genes] = jnp.sum(jnp.where(listed(i), sums, 0.0), axis=0, keepdims=True)

        def query_step(step, carry):
            n = wide_at(step)
            across = nn_dot(kt[...], low[n])
            dq[wide_of(n), :] = (across.T * scale).astype(BF16)

            @pl.when(step > 0)
            def _():
                give_wide_back(0, dq, dq_out, step - 1, wides // 2, 4)

            @pl.when(step == 0)
            def _():
                for to_step in range(genes):
                    to = peer(to_step)[2]
                    pltpu.make_async_remote_copy(
                        src_ref=terms.at[to],
                        dst_ref=mine.at[1 - half, head],
                        send_sem=term_send.at[0],
                        recv_sem=term_recv,
                        device_id=device_at(to),
                        device_id_type=MESH,
                    ).start()
                    if to_step > 0:
                        pltpu.make_async_remote_copy(
                            src_ref=terms.at[to],
                            dst_ref=mine.at[1 - half, head],
                            send_sem=term_send.at[1],
                            recv_sem=term_recv,
                            device_id={"gene": to},
                            device_id_type=MESH,
                        ).start()
                pltpu.make_async_copy(terms.at[gene], mine.at[1 - half, head], term_recv).start()

            return carry

        lax.fori_loop(0, wides, query_step, 0)
        give_wide_back(0, dq, dq_out, wides - 1, wides // 2, 4)

        def key_step(step, carry):
            m = early_at(step)
            dk[wide_of(m), :] = (over_queries(m, qf) * scale).astype(BF16)

            @pl.when(step > 0)
            def _():
                give_keys(step - 1)

            return carry

        lax.fori_loop(0, wides, key_step, 0)
        give_keys(wides - 1)
    @pl.when(jnp.logical_not(active))
    def _():
        for part in range(4):
            pass_on(2, dv_out, part, part * lap)
        for part in range(2):
            pass_on(0, dq_out, 4 + part, part * lap)

    square[...] = jnp.zeros_like(square)
    arrived(mine, term_recv)
    own_place = cell // 4 * 2 + core
    for step in range(1, cells // 2):
        pltpu.make_async_remote_copy(
            src_ref=mine,
            dst_ref=everyones.at[own_place],
            send_sem=cell_send,
            recv_sem=cell_recv,
            device_id={"cell": alike(step)},
            device_id_type=MESH,
        ).start()
    pltpu.make_async_copy(mine, everyones.at[own_place], cell_recv).start()
    arrived(everyones, cell_recv)
    everything = jnp.sum(everyones[...], axis=(0, 1))
    for h in range(heads):
        square[h : h + 1, :] = everything[h]
    slot_rows = lax.broadcasted_iota(jnp.int32, (BLOCK, BLOCK), 0)
    picked = jnp.sum(jnp.where(slot_rows == cell, square[...].T, 0.0), axis=0, keepdims=True)
    bias_out[0] = picked[:, 0:heads]

    for a, out in enumerate((dq_out, dk_out, dv_out)):
        arrived(out, out_recv.at[a])

    def sent(ref, count, sem):
        part = ref.at[pl.ds(0, count)]
        pltpu.make_async_copy(part, part, sem).wait()

    for a in range(4):
        sent(kf, heads * BLOCK, in_send.at[a])
    sent(statf, heads, in_send.at[4])

    @pl.when(active)
    def _():
        for a in range(3):
            sent(dq, genes * BLOCK, out_send.at[a])
        sent(terms, genes, term_send.at[0])
        sent(terms, genes - 1, term_send.at[1])

    @pl.when(jnp.logical_not(active))
    def _():
        sent(dv, genes * BLOCK, out_send.at[2])
        sent(dq, genes // 2 * BLOCK, out_send.at[0])

    sent(everyones, cells // 2 - 1, cell_send)


def put_out(*refs):
    count = (len(refs) - 1) // 2
    copies = [
        pltpu.make_async_copy(refs[n], refs[count + n], refs[-1].at[n]) for n in range(count)
    ]
    for copy in copies:
        copy.start()
    for copy in copies:
        copy.wait()


def shards(
    query_rows,
    key_rows,
    value_rows,
    output_rows,
    output_grad,
    row_lse,
    block_bias,
    block_index,
    block_count,
):
    heads = row_lse.shape[2]
    genes = block_index.shape[0]
    cells = lax.axis_size("cell")
    rows = genes * BLOCK
    anywhere = pl.BlockSpec(memory_space=pl.ANY)
    vmem = pl.BlockSpec(memory_space=pltpu.VMEM)
    flat = jax.ShapeDtypeStruct(query_rows.shape, BF16)
    dma = pltpu.SemaphoreType.DMA
    wides = rows // WIDE
    held = pltpu.VMEM(query_rows.shape, BF16)
    bias_flat = (1, 1, heads)
    results = pl.pallas_call(
        functools.partial(kernel, heads, genes, cells),
        out_shape=(held, held, held, pltpu.VMEM(bias_flat, F32)),
        in_specs=[pl.BlockSpec(memory_space=pltpu.HBM)] * 9,
        out_specs=(vmem, vmem, vmem, vmem),
        scratch_shapes=[
            pltpu.VMEM((rows, BLOCK), BF16),
            pltpu.VMEM((rows, BLOCK), BF16),
            pltpu.VMEM((rows, BLOCK), BF16),
            pltpu.VMEM((rows, BLOCK), BF16),
            pltpu.VMEM((genes, 2, BLOCK), F32),
            pltpu.VMEM((BLOCK, heads * BLOCK), BF16),
            pltpu.VMEM((BLOCK, heads * BLOCK), BF16),
            pltpu.VMEM((heads, 2, BLOCK), F32),
            pltpu.VMEM((BLOCK, BLOCK), F32),
            pltpu.VMEM((BLOCK, rows), BF16),
            pltpu.VMEM((wides, genes, WIDE), F32),
            pltpu.VMEM((wides, rows, WIDE), F32),
            pltpu.VMEM((wides, rows, WIDE), BF16),
            pltpu.VMEM((wides, genes, WIDE), F32),
            pltpu.VMEM((rows, BLOCK), BF16),
            pltpu.VMEM((rows, BLOCK), BF16),
            pltpu.VMEM((rows, BLOCK), BF16),
            pltpu.VMEM((genes, 1, BLOCK), F32),
            pltpu.VMEM((2, heads, 1, BLOCK), F32),
            pltpu.VMEM((cells // 2, 2, heads, 1, BLOCK), F32),
            pltpu.VMEM((6, RELAYED * BLOCK, BLOCK), BF16),
            pltpu.VMEM((heads, 1, BLOCK), F32),
            pltpu.VMEM((heads, genes, genes), F32),
            pltpu.VMEM((genes, genes), jnp.int32),
            pltpu.SMEM((genes,), jnp.int32),
            dma((6,)),
            dma((5,)),
            dma((5,)),
            dma((SIDE,)),
            dma((3,)),
            dma((3,)),
            dma((6,)),
            dma((2,)),
            dma,
            dma,
            dma,
        ],
        compiler_params=pltpu.CompilerParams(
            collective_id=0, has_side_effects=True, vmem_limit_bytes=60 * 1024 * 1024
        ),
    )(
        query_rows,
        key_rows,
        value_rows,
        output_rows,
        output_grad,
        jnp.transpose(row_lse, (2, 0, 1)),
        jnp.transpose(block_bias, (1, 0, 2)),
        block_index,
        block_count,
    )
    query_grad, key_grad, value_grad, bias_grad = pl.pallas_call(
        put_out,
        out_shape=(flat, flat, flat, jax.ShapeDtypeStruct(bias_flat, F32)),
        in_specs=[anywhere] * 4,
        out_specs=(anywhere,) * 4,
        scratch_shapes=[dma((4,))],
        compiler_params=pltpu.CompilerParams(vmem_limit_bytes=1024 * 1024),
    )(*(pltpu.with_memory_space_constraint(r, pltpu.VMEM) for r in results))
    return (query_grad, key_grad, value_grad, jnp.transpose(bias_grad, (0, 2, 1)))


def solution(mesh):
    in_specs = (
        P("cell", "gene", None),
        P("cell", "gene", None),
        P("cell", "gene", None),
        P("cell", "gene", None),
        P("cell", "gene", None),
        P("cell", "gene", None),
        P(),
        P(),
        P(),
    )
    out_specs = (
        P("cell", "gene", None),
        P("cell", "gene", None),
        P("cell", "gene", None),
        P("gene", None, "cell"),
    )
    return jax.shard_map(shards, mesh=mesh, in_specs=in_specs, out_specs=out_specs, check_vma=False)
```
